32 devices in a mesh: dp: 8 (over y, x, core), tensor: 4 (over z).
Axes of the slice: x: 2, y: 2, z: 4, core: 2. Of those that a mesh axis runs over, the one named last changes fastest.
Arguments:
- frames: bfloat16 [16, 256, 1536], P('dp', 'tensor'), may hold values from -6 to 6
- text_states: bfloat16 [16, 64, 1536], P('dp', 'tensor'), may hold values from -6 to 6
- self_q: bfloat16 [1536, 1536], P('dp', 'tensor'), may hold values from -0.15625 to 0.15625
- self_k: bfloat16 [1536, 1536], P('dp', 'tensor'), may hold values from -0.15625 to 0.15625
- self_v: bfloat16 [1536, 1536], P('dp', 'tensor'), may hold values from -0.15625 to 0.15625
- self_out: bfloat16 [1536, 1536], P('tensor', 'dp'), may hold values from -1.25 to 1.25
- cross_q: bfloat16 [1536, 1536], P('dp', 'tensor'), may hold values from -0.15625 to 0.15625
- cross_k: bfloat16 [1536, 1536], P('dp', 'tensor'), may hold values from -0.15625 to 0.15625
- cross_v: bfloat16 [1536, 1536], P('dp', 'tensor'), may hold values from -0.15625 to 0.15625
- cross_out: bfloat16 [1536, 1536], P('tensor', 'dp'), may hold values from -0.625 to 0.625
- mlp_up: bfloat16 [1536, 6144], P('dp', 'tensor'), may hold values from -0.15625 to 0.15625
- mlp_down: bfloat16 [6144, 1536], P('tensor', 'dp'), may hold values from -0.3125 to 0.3125
- norm_gains: float32 [3, 1536], P(None, ('dp', 'tensor')), may hold values from 0.5 to 1.5
- norm_shifts: float32 [3, 1536], P(None, ('dp', 'tensor')), may hold values from -3 to 3
- cotangent: bfloat16 [16, 256, 1536], P('dp', 'tensor'), may hold values from -6 to 6
Outputs:
- activations: bfloat16 [16, 256, 1536], P('dp', 'tensor')
- grad_frames: float32 [16, 256, 1536], P('dp', 'tensor')
- grad_text: float32 [16, 64, 1536], P('dp', 'tensor')
- grad_self_q: float32 [1536, 1536], P('dp', 'tensor')
- grad_self_k: float32 [1536, 1536], P('dp', 'tensor')
- grad_self_v: float32 [1536, 1536], P('dp', 'tensor')
- grad_self_out: float32 [1536, 1536], P('tensor', 'dp')
- grad_cross_q: float32 [1536, 1536], P('dp', 'tensor')
- grad_cross_k: float32 [1536, 1536], P('dp', 'tensor')
- grad_cross_v: float32 [1536, 1536], P('dp', 'tensor')
- grad_cross_out: float32 [1536, 1536], P('tensor', 'dp')
- grad_mlp_up: float32 [1536, 6144], P('dp', 'tensor')
- grad_mlp_down: float32 [6144, 1536], P('tensor', 'dp')
- grad_norm_gains: float32 [3, 1536], P(None, ('dp', 'tensor'))
- grad_norm_shifts: float32 [3, 1536], P(None, ('dp', 'tensor'))
The draws below stay inside these ranges and needn't reach their ends.
All inputs are finite; a program needn't handle non-finite values.
Results may differ from the reference program's by a relative error of at most 0.028.
Values may be sent and summed in bfloat16 or wider, within the bound.
No kernel may reach another device: no remote copies, remote signals or barrier semaphores. Data moves between devices by JAX's collectives and lax.ppermute only.
A program may use at most 192 MiB of HBM per device.

```python
import math
import jax
import jax.numpy as jnp
from jax import lax

D = 1536
HEADS = 24
HEAD_DIM = 64
FF = 6144
TEXT = 64
SEQ = 256
SEQS = 16


def raised(drawn, own_key, source, target, parts, factor):
    owner, partner = [(jnp.arange(drawn.shape[dim]) // (drawn.shape[dim] // parts)).reshape([-1 if axis == dim else 1 for axis in range(drawn.ndim)]) for dim in (source, target)]
    chosen = jax.random.permutation(own_key, parts)[partner]
    strong = (owner == chosen) | (owner == (partner + parts // 2) % parts)
    return jnp.where(strong, factor * drawn, drawn)


def block_levels(stream_key, extent, shards, least, largest):
    level, own = 1.0, jax.random.fold_in(stream_key, 6)
    for dim, parts in shards:
        heights = jnp.exp(jax.random.uniform(jax.random.fold_in(own, dim), (parts,), jnp.float32, least / len(shards), largest / len(shards)))
        level = level * jnp.repeat(heights, extent[dim] // parts).reshape([-1 if axis == dim else 1 for axis in range(len(extent))])
    return level


def gaussian(stream_key, shape, deviation, bound, pieces=(), kind=jnp.bfloat16):
    drawn = deviation * jax.random.normal(stream_key, shape, jnp.float32)
    if pieces:
        drawn = drawn * block_levels(stream_key, shape, pieces, -0.22, 0.18)
    return jnp.clip(drawn, -bound, bound).astype(kind)


def gaussian_with(rng, shape, deviation, reach, pieces, heavy, held_as=jnp.bfloat16):
    drawn = deviation * jax.random.normal(rng, shape, jnp.float32)
    if pieces:
        drawn = drawn * block_levels(rng, shape, pieces, -0.22, 0.18)
    return jnp.clip(raised(drawn, jax.random.fold_in(rng, 3), *heavy), -reach, reach).astype(held_as)


def setup_inputs(seed: int = 0) -> dict:
    seeds = jax.random.split(jax.random.key(seed), 16)
    frames = gaussian(seeds[0], (SEQS, SEQ, D), 1.0, 6.0, ((0, 8), (1, 4)))
    text_states = gaussian(seeds[1], (SEQS, TEXT, D), 1.0, 6.0, ((0, 8), (1, 4)))
    self_q = gaussian(seeds[2], (D, D), D ** -0.5, 0.15625, ((0, 8), (1, 4)))
    self_k = gaussian(seeds[3], (D, D), D ** -0.5, 0.15625, ((0, 8), (1, 4)))
    self_v = gaussian(seeds[4], (D, D), D ** -0.5, 0.15625, ((0, 8), (1, 4)))
    self_out = gaussian(seeds[5], (D, D), (D // 64) ** -0.5, 1.25, ((0, 4), (1, 8)))
    cross_q = gaussian(seeds[6], (D, D), D ** -0.5, 0.15625, ((0, 8), (1, 4)))
    cross_k = gaussian(seeds[7], (D, D), D ** -0.5, 0.15625, ((0, 8), (1, 4)))
    cross_v = gaussian(seeds[8], (D, D), D ** -0.5, 0.15625, ((0, 8), (1, 4)))
    cross_out = gaussian(seeds[9], (D, D), (D // 16) ** -0.5, 0.625, ((0, 4), (1, 8)))
    mlp_up = gaussian(seeds[10], (D, FF), D ** -0.5, 0.15625, ((0, 8), (1, 4)))
    mlp_down = gaussian(seeds[11], (FF, D), (FF // 16) ** -0.5, 0.3125, ((0, 4), (1, 8)))
    norm_gains = jnp.clip(1.0 + 0.1 * jax.random.normal(seeds[12], (3, D), jnp.float32), 0.5, 1.5)
    norm_shifts = gaussian(seeds[13], (3, D), 0.5, 3.0, ((1, 32),), jnp.float32)
    cotangent = gaussian_with(seeds[14], (SEQS, SEQ, D), 1.0, 6.0, ((0, 8), (1, 4)), (0, 2, 8, 2.0))
    return {"frames": frames, "text_states": text_states, "self_q": self_q, "self_k": self_k, "self_v": self_v, "self_out": self_out, "cross_q": cross_q, "cross_k": cross_k, "cross_v": cross_v, "cross_out": cross_out, "mlp_up": mlp_up, "mlp_down": mlp_down, "norm_gains": norm_gains, "norm_shifts": norm_shifts, "cotangent": cotangent}


@jax.custom_vjp
def low(v):
    return lax.optimization_barrier(v.astype(jnp.bfloat16)).astype(jnp.float32)

@jax.custom_vjp
def low_back(v):
    return v

def low_keep(v):
    return (low(v), None)

def low_pass(kept, grad):
    return (grad,)

def back_keep(v):
    return (v, None)

def back_low(kept, grad):
    return (low(grad),)
low.defvjp(low_keep, low_pass)
low_back.defvjp(back_keep, back_low)
EPS = 1e-05
HIGHEST = lax.Precision.HIGHEST

def lowered(values):
    return low(low_back(values))

def layer_norm(values, gain, shift):
    average = lax.optimization_barrier(jnp.mean(values, axis=-1, keepdims=True))
    centered = values - average
    variance = lax.optimization_barrier(jnp.mean(centered * centered, axis=-1, keepdims=True))
    return centered * lax.rsqrt(variance + EPS) * gain + shift

def project(operand, matrix):
    return jnp.einsum('gsd,de->gse', operand, matrix, precision=HIGHEST)

def attend_one(queries, key_rows, value_rows, causal):
    query_count = queries.shape[0]
    key_count = key_rows.shape[0]
    heads_query = queries.reshape(query_count, HEADS, HEAD_DIM)
    heads_key = key_rows.reshape(key_count, HEADS, HEAD_DIM)
    heads_value = value_rows.reshape(key_count, HEADS, HEAD_DIM)
    scores = jnp.einsum('qhd,khd->hqk', heads_query, heads_key, precision=HIGHEST) * HEAD_DIM ** (-0.5)
    scores = low_back(scores)
    if causal:
        visible = jnp.arange(query_count)[:, None] >= jnp.arange(key_count)[None, :]
        scores = jnp.where(visible[None, :, :], scores, -1e+30)
    probability = low(jax.nn.softmax(scores, axis=-1))
    mixture = jnp.einsum('hqk,khd->qhd', probability, heads_value, precision=HIGHEST)
    return lowered(mixture.reshape(query_count, HEADS * HEAD_DIM))

def self_block(members):
    return attend_one(members[0], members[1], members[2], True)

def cross_block(members):
    return attend_one(members[0], members[1], members[2], False)

def forward(weights, frames, text_states):
    self_q, self_k, self_v, self_out, cross_q, cross_k, cross_v, cross_out, mlp_up, mlp_down, gain_rows, shifts = weights
    normed_self = low(layer_norm(frames, gain_rows[0], shifts[0]))
    query_self = lowered(project(normed_self, self_q))
    key_self = lowered(project(normed_self, self_k))
    value_self = lowered(project(normed_self, self_v))
    mixture_self = lax.map(jax.checkpoint(self_block), (query_self, key_self, value_self))
    resid_self = frames + low_back(project(mixture_self, self_out))
    normed_cross = low(layer_norm(resid_self, gain_rows[1], shifts[1]))
    query_cross = lowered(project(normed_cross, cross_q))
    key_cross = lowered(project(text_states, cross_k))
    value_cross = lowered(project(text_states, cross_v))
    mixture_cross = lax.map(jax.checkpoint(cross_block), (query_cross, key_cross, value_cross))
    resid_cross = resid_self + low_back(project(mixture_cross, cross_out))
    normed_mlp = low(layer_norm(resid_cross, gain_rows[2], shifts[2]))
    hidden = low_back(project(normed_mlp, mlp_up))
    active = low(jax.nn.gelu(hidden, approximate=False))
    return resid_cross + low_back(project(active, mlp_down))

def add_pair(first_term, second_term):
    return first_term + second_term

def reference(frames, text_states, self_q, self_k, self_v, self_out, cross_q, cross_k, cross_v, cross_out, mlp_up, mlp_down, norm_gains, norm_shifts, cotangent):
    weights = (self_q.astype(jnp.float32), self_k.astype(jnp.float32), self_v.astype(jnp.float32), self_out.astype(jnp.float32), cross_q.astype(jnp.float32), cross_k.astype(jnp.float32), cross_v.astype(jnp.float32), cross_out.astype(jnp.float32), mlp_up.astype(jnp.float32), mlp_down.astype(jnp.float32), norm_gains.astype(jnp.float32), norm_shifts.astype(jnp.float32))
    group_size = math.gcd(SEQS, max(1, 4096 // SEQ))
    group_count = SEQS // group_size
    frame_blocks = frames.astype(jnp.float32).reshape(group_count, group_size, SEQ, D)
    text_blocks = text_states.astype(jnp.float32).reshape(group_count, group_size, TEXT, D)
    cotangent_blocks = cotangent.astype(jnp.float32).reshape(group_count, group_size, SEQ, D)

    def visit(totals, members):
        result, pullback = jax.vjp(forward, weights, members[0], members[1])
        grad_weights, grad_input, grad_words = pullback(members[2])
        totals = jax.tree.map(add_pair, totals, grad_weights)
        return (totals, (result.astype(jnp.bfloat16), grad_input, grad_words))
    initial = jax.tree.map(jnp.zeros_like, weights)
    totals, (outputs, grad_input, grad_words) = lax.scan(visit, initial, (frame_blocks, text_blocks, cotangent_blocks))
    return (outputs.reshape(SEQS, SEQ, D), grad_input.reshape(SEQS, SEQ, D), grad_words.reshape(SEQS, TEXT, D), totals[0], totals[1], totals[2], totals[3], totals[4], totals[5], totals[6], totals[7], totals[8], totals[9], totals[10], totals[11])
```

```python
import jax
import jax.numpy as jnp
from jax import lax
from jax.sharding import PartitionSpec as P

HEAD_DIM = 64
EPS = 1e-05
LOW = jnp.bfloat16
WIDE = jnp.float32


def norm_forward(values, gain, shift):
    average = jnp.mean(values, axis=-1, keepdims=True)
    centered = values - average
    variance = jnp.mean(centered * centered, axis=-1, keepdims=True)
    inverse = lax.rsqrt(variance + EPS)
    unit = centered * inverse
    return unit * gain + shift, unit, inverse


def norm_back(unit, inverse, gain, upstream):
    scaled = upstream * gain
    mean_scaled = jnp.mean(scaled, axis=-1, keepdims=True)
    mean_product = jnp.mean(scaled * unit, axis=-1, keepdims=True)
    change = inverse * (scaled - mean_scaled - unit * mean_product)
    return change, jnp.sum(upstream * unit, axis=0), jnp.sum(upstream, axis=0)


def gelu_exact(values):
    return jax.nn.gelu(values, approximate=False)


def product(operand, matrix):
    return jnp.dot(operand, matrix, preferred_element_type=WIDE)


def product_left(operand, matrix):
    return lax.dot_general(operand, matrix, (((0,), (0,)), ((), ())), preferred_element_type=WIDE)


def product_right(operand, matrix):
    return lax.dot_general(operand, matrix, (((1,), (1,)), ((), ())), preferred_element_type=WIDE)


def swap(value, axis, stride):
    size = lax.axis_size(axis)
    return lax.ppermute(value, axis, [(i, i ^ stride) for i in range(size)])


def levels():
    found, stride = [], 1
    for axis in ("tensor", "dp"):
        step = 1
        while step < lax.axis_size(axis):
            found.append((axis, step))
            step *= 2
    return found


def gather_small(value):
    for axis, step in levels():
        upper = (lax.axis_index(axis) // step) % 2 == 1
        other = swap(value, axis, step)
        value = jnp.where(
            upper,
            jnp.concatenate([other, value], axis=-1),
            jnp.concatenate([value, other], axis=-1),
        )
    return value


def scatter_small(value):
    for axis, step in reversed(levels()):
        upper = (lax.axis_index(axis) // step) % 2 == 1
        half = value.shape[-1] // 2
        low, high = value[..., :half], value[..., half:]
        other = swap(jnp.where(upper, low, high), axis, step)
        value = jnp.where(upper, high, low) + other
    return value


def spread(local):
    gathered = lax.all_gather(local, "tensor", axis=0, tiled=False)
    return gathered.reshape(-1, local.shape[-1])


def collect(partial, shape):
    summed = lax.psum_scatter(
        partial.astype(LOW), "tensor", scatter_dimension=0, tiled=True
    )
    return summed.astype(WIDE)


def by_heads(rows, count, seqs):
    frames = rows.shape[0] // (count * seqs)
    split = rows.reshape(count, seqs, frames, -1, HEAD_DIM)
    return split.transpose(1, 3, 0, 2, 4).reshape(seqs, -1, count * frames, HEAD_DIM)


def by_rows(heads, count, seqs):
    frames = heads.shape[2] // count
    split = heads.reshape(seqs, heads.shape[1], count, frames, HEAD_DIM)
    return split.transpose(2, 0, 3, 1, 4).reshape(count * seqs * frames, -1)


def weights_of(queries, keys, causal):
    scores = jnp.einsum("shqd,shkd->shqk", queries, keys, preferred_element_type=WIDE)
    scores = scores * HEAD_DIM**-0.5
    if causal:
        length = queries.shape[2]
        visible = jnp.arange(length)[:, None] >= jnp.arange(length)[None, :]
        scores = jnp.where(visible, scores, -1e30)
    largest = jnp.max(scores, axis=-1, keepdims=True)
    raw = jnp.exp(scores - largest)
    return raw / jnp.sum(raw, axis=-1, keepdims=True)


def attend(queries, keys, values, causal):
    chance = weights_of(queries, keys, causal).astype(LOW)
    return jnp.einsum("shqk,shkd->shqd", chance, values, preferred_element_type=WIDE).astype(LOW)


def attend_back(queries, keys, values, upstream, causal):
    chance = weights_of(queries, keys, causal)
    grad = jnp.einsum("shqd,shkd->shqk", upstream, values, preferred_element_type=WIDE)
    dots = jnp.sum(chance * grad, axis=-1, keepdims=True)
    score_grad = (chance * (grad - dots)).astype(LOW)
    scaling = HEAD_DIM**-0.5
    grad_q = jnp.einsum("shqk,shkd->shqd", score_grad, keys, preferred_element_type=WIDE)
    grad_k = jnp.einsum("shqk,shqd->shkd", score_grad, queries, preferred_element_type=WIDE)
    grad_v = jnp.einsum("shqk,shqd->shkd", chance.astype(LOW), upstream, preferred_element_type=WIDE)
    return (grad_q * scaling).astype(LOW), (grad_k * scaling).astype(LOW), grad_v.astype(LOW)


def on_device(
    frames,
    text_states,
    self_q,
    self_k,
    self_v,
    self_out,
    cross_q,
    cross_k,
    cross_v,
    cross_out,
    mlp_up,
    mlp_down,
    norm_gains,
    norm_shifts,
    cotangent,
):
    seqs, own, width = frames.shape
    text_own = text_states.shape[1]
    count = lax.axis_size("tensor")
    inner = self_q.shape[1]

    norms = gather_small(jnp.concatenate([norm_gains, norm_shifts], axis=0))
    gains, shifts = norms[:3], norms[3:]

    whole_grad = spread(cotangent.reshape(-1, width))
    whole_text = spread(text_states.reshape(-1, width))

    def gather(parts):
        joined = parts[0] if len(parts) == 1 else jnp.concatenate(parts, axis=1)
        return lax.all_gather(joined, "dp", axis=0, tiled=True)

    full_qkv = gather([self_q, self_k, self_v])
    full_mid = gather([self_out.T, cross_q, cross_k, cross_v, cross_out.T])
    full_mlp = gather([mlp_up, mlp_down.T])
    full_out = full_mid[:, :inner]
    full_cq = full_mid[:, inner : 2 * inner]
    full_ckv = full_mid[:, 2 * inner : 4 * inner]
    full_cout = full_mid[:, 4 * inner :]
    hidden_own = mlp_up.shape[1]
    full_up, full_down = full_mlp[:, :hidden_own], full_mlp[:, hidden_own:]

    x0 = frames.reshape(-1, width).astype(WIDE)
    a1, unit0, inverse0 = norm_forward(x0, gains[0], shifts[0])
    whole_self = spread(a1.astype(LOW))
    qkv = product(whole_self, full_qkv).astype(LOW)
    query1 = by_heads(qkv[:, :inner], count, seqs)
    key1 = by_heads(qkv[:, inner : 2 * inner], count, seqs)
    value1 = by_heads(qkv[:, 2 * inner :], count, seqs)
    mix1 = by_rows(attend(query1, key1, value1, True), count, seqs)
    x1 = x0 + collect(product_right(mix1, full_out), None)

    a2, unit1, inverse1 = norm_forward(x1, gains[1], shifts[1])
    whole_cross = spread(a2.astype(LOW))
    query2 = by_heads(product(whole_cross, full_cq).astype(LOW), count, seqs)
    text_kv = product(whole_text, full_ckv).astype(LOW)
    key2 = by_heads(text_kv[:, :inner], count, seqs)
    value2 = by_heads(text_kv[:, inner:], count, seqs)
    mix2 = by_rows(attend(query2, key2, value2, False), count, seqs)
    x2 = x1 + collect(product_right(mix2, full_cout), None)

    a3, unit2, inverse2 = norm_forward(x2, gains[2], shifts[2])
    whole_mlp = spread(a3.astype(LOW))
    hidden = product(whole_mlp, full_up)
    active_grad = product(whole_grad, full_down)
    active, pullback = jax.vjp(gelu_exact, hidden)
    active = active.astype(LOW)
    hidden_low = pullback(active_grad)[0].astype(LOW)
    h3 = collect(product_right(hidden_low, full_up), None)
    activations = (x2 + collect(product_right(active, full_down), None)).astype(LOW)

    def reduce(parts):
        joined = parts[0] if len(parts) == 1 else jnp.concatenate(parts, axis=1)
        return lax.psum_scatter(joined, "dp", scatter_dimension=0, tiled=True).astype(WIDE)

    sum_mlp = reduce(
        [
            product_left(whole_mlp, hidden_low).astype(LOW),
            product_left(whole_grad, active).astype(LOW),
        ]
    )

    e3 = cotangent.reshape(-1, width).astype(WIDE)
    change, gain2, shift2 = norm_back(unit2, inverse2, gains[2], h3)
    e2 = e3 + change
    whole_c2 = spread(e2.astype(LOW))
    d2 = by_heads(product(whole_c2, full_cout).astype(LOW), count, seqs)
    grad_q2, grad_k2, grad_v2 = attend_back(query2, key2, value2, d2, False)
    grad_q2 = by_rows(grad_q2, count, seqs)
    grad_kv2 = jnp.concatenate(
        [by_rows(grad_k2, count, seqs), by_rows(grad_v2, count, seqs)], axis=1
    )
    h2 = collect(product_right(grad_q2, full_cq), None)
    grad_text = collect(product_right(grad_kv2, full_ckv), None)
    sum_cross = reduce(
        [
            product_left(whole_cross, grad_q2).astype(LOW),
            product_left(whole_text, grad_kv2).astype(LOW),
            product_left(whole_c2, mix2).astype(LOW),
        ]
    )

    change, gain1, shift1 = norm_back(unit1, inverse1, gains[1], h2)
    e1 = e2 + change
    whole_c1 = spread(e1.astype(LOW))
    d1 = by_heads(product(whole_c1, full_out).astype(LOW), count, seqs)
    grads = attend_back(query1, key1, value1, d1, True)
    grad_qkv = jnp.concatenate([by_rows(part, count, seqs) for part in grads], axis=1)
    h1 = collect(product_right(grad_qkv, full_qkv), None)
    sum_self = reduce(
        [
            product_left(whole_self, grad_qkv).astype(LOW),
            product_left(whole_c1, mix1).astype(LOW),
        ]
    )
    change, gain0, shift0 = norm_back(unit0, inverse0, gains[0], h1)
    grad_frames = e1 + change

    norm_sums = scatter_small(jnp.stack([gain0, gain1, gain2, shift0, shift1, shift2]))

    def cut(joined, index):
        return joined[:, index * inner : (index + 1) * inner]

    return (
        activations.reshape(frames.shape),
        grad_frames.reshape(frames.shape),
        grad_text.reshape(text_states.shape),
        cut(sum_self, 0),
        cut(sum_self, 1),
        cut(sum_self, 2),
        cut(sum_self, 3).T,
        cut(sum_cross, 0),
        cut(sum_cross, 1),
        cut(sum_cross, 2),
        cut(sum_cross, 3).T,
        sum_mlp[:, :hidden_own],
        sum_mlp[:, hidden_own:].T,
        norm_sums[:3],
        norm_sums[3:],
    )


def solution(mesh):
    rows = P("dp", "tensor", None)
    into = P("dp", "tensor")
    out_of = P("tensor", "dp")
    norms = P(None, ("dp", "tensor"))
    weights = (into, into, into, out_of, into, into, into, out_of, into, out_of)
    return jax.shard_map(
        on_device,
        mesh=mesh,
        in_specs=(rows, rows, *weights, norms, norms, rows),
        out_specs=(rows, rows, rows, *weights, norms, norms),
        check_vma=False,
    )
```

```python
import functools

import jax
import jax.numpy as jnp
from jax import lax
from jax.experimental import pallas as pl
from jax.sharding import PartitionSpec as P

HEAD_DIM = 64
EPS = 1e-05
LOW = jnp.bfloat16
WIDE = jnp.float32


def norm_forward(values, gain, shift):
    average = jnp.mean(values, axis=-1, keepdims=True)
    centered = values - average
    variance = jnp.mean(centered * centered, axis=-1, keepdims=True)
    inverse = lax.rsqrt(variance + EPS)
    unit = centered * inverse
    return unit * gain + shift, unit, inverse


def norm_back(unit, inverse, gain, upstream):
    scaled = upstream * gain
    mean_scaled = jnp.mean(scaled, axis=-1, keepdims=True)
    mean_product = jnp.mean(scaled * unit, axis=-1, keepdims=True)
    change = inverse * (scaled - mean_scaled - unit * mean_product)
    return change, jnp.sum(upstream * unit, axis=0), jnp.sum(upstream, axis=0)


def gelu_exact(values):
    return jax.nn.gelu(values, approximate=False)


def product(operand, matrix):
    return jnp.dot(operand, matrix, preferred_element_type=WIDE)


def product_left(operand, matrix):
    return lax.dot_general(operand, matrix, (((0,), (0,)), ((), ())), preferred_element_type=WIDE)


def product_right(operand, matrix):
    return lax.dot_general(operand, matrix, (((1,), (1,)), ((), ())), preferred_element_type=WIDE)


def swap(value, axis, stride):
    size = lax.axis_size(axis)
    return lax.ppermute(value, axis, [(i, i ^ stride) for i in range(size)])


def levels():
    found, stride = [], 1
    for axis in ("tensor", "dp"):
        step = 1
        while step < lax.axis_size(axis):
            found.append((axis, step))
            step *= 2
    return found


def gather_small(value):
    for axis, step in levels():
        upper = (lax.axis_index(axis) // step) % 2 == 1
        other = swap(value, axis, step)
        value = jnp.where(
            upper,
            jnp.concatenate([other, value], axis=-1),
            jnp.concatenate([value, other], axis=-1),
        )
    return value


def scatter_small(value):
    for axis, step in reversed(levels()):
        upper = (lax.axis_index(axis) // step) % 2 == 1
        half = value.shape[-1] // 2
        low, high = value[..., :half], value[..., half:]
        other = swap(jnp.where(upper, low, high), axis, step)
        value = jnp.where(upper, high, low) + other
    return value


def spread(local):
    gathered = lax.all_gather(local, "tensor", axis=0, tiled=False)
    return gathered.reshape(-1, local.shape[-1])


def collect(partial, shape):
    summed = lax.psum_scatter(
        partial.astype(LOW), "tensor", scatter_dimension=0, tiled=True
    )
    return summed.astype(WIDE)


def by_heads(rows, count, seqs):
    frames = rows.shape[0] // (count * seqs)
    split = rows.reshape(count, seqs, frames, -1, HEAD_DIM)
    return split.transpose(1, 3, 0, 2, 4).reshape(seqs, -1, count * frames, HEAD_DIM)


def by_rows(heads, count, seqs):
    frames = heads.shape[2] // count
    split = heads.reshape(seqs, heads.shape[1], count, frames, HEAD_DIM)
    return split.transpose(2, 0, 3, 1, 4).reshape(count * seqs * frames, -1)


def weights_of(queries, keys, causal):
    scores = jnp.einsum("shqd,shkd->shqk", queries, keys, preferred_element_type=WIDE)
    scores = scores * HEAD_DIM**-0.5
    if causal:
        length = queries.shape[2]
        visible = jnp.arange(length)[:, None] >= jnp.arange(length)[None, :]
        scores = jnp.where(visible, scores, -1e30)
    largest = jnp.max(scores, axis=-1, keepdims=True)
    raw = jnp.exp(scores - largest)
    return raw / jnp.sum(raw, axis=-1, keepdims=True)


def attend(queries, keys, values, causal):
    chance = weights_of(queries, keys, causal).astype(LOW)
    return jnp.einsum("shqk,shkd->shqd", chance, values, preferred_element_type=WIDE).astype(LOW)


def attend_back(queries, keys, values, upstream, causal):
    chance = weights_of(queries, keys, causal)
    grad = jnp.einsum("shqd,shkd->shqk", upstream, values, preferred_element_type=WIDE)
    dots = jnp.sum(chance * grad, axis=-1, keepdims=True)
    score_grad = (chance * (grad - dots)).astype(LOW)
    scaling = HEAD_DIM**-0.5
    grad_q = jnp.einsum("shqk,shkd->shqd", score_grad, keys, preferred_element_type=WIDE)
    grad_k = jnp.einsum("shqk,shqd->shkd", score_grad, queries, preferred_element_type=WIDE)
    grad_v = jnp.einsum("shqk,shqd->shkd", chance.astype(LOW), upstream, preferred_element_type=WIDE)
    return (grad_q * scaling).astype(LOW), (grad_k * scaling).astype(LOW), grad_v.astype(LOW)


def on_device(
    frames,
    text_states,
    self_q,
    self_k,
    self_v,
    self_out,
    cross_q,
    cross_k,
    cross_v,
    cross_out,
    mlp_up,
    mlp_down,
    norm_gains,
    norm_shifts,
    cotangent,
):
    seqs, own, width = frames.shape
    text_own = text_states.shape[1]
    count = lax.axis_size("tensor")
    inner = self_q.shape[1]

    norms = gather_small(jnp.concatenate([norm_gains, norm_shifts], axis=0))
    gains, shifts = norms[:3], norms[3:]

    whole_grad = spread(cotangent.reshape(-1, width))
    whole_text = spread(text_states.reshape(-1, width))

    def gather(parts):
        joined = parts[0] if len(parts) == 1 else jnp.concatenate(parts, axis=1)
        return lax.all_gather(joined, "dp", axis=0, tiled=True)

    full_qkv = gather([self_q, self_k, self_v])
    full_mid = gather([self_out.T, cross_q, cross_k, cross_v, cross_out.T])
    full_mlp = gather([mlp_up, mlp_down.T])
    full_out = full_mid[:, :inner]
    full_cq = full_mid[:, inner : 2 * inner]
    full_ckv = full_mid[:, 2 * inner : 4 * inner]
    full_cout = full_mid[:, 4 * inner :]
    hidden_own = mlp_up.shape[1]
    full_up, full_down = full_mlp[:, :hidden_own], full_mlp[:, hidden_own:]

    x0 = frames.reshape(-1, width).astype(WIDE)
    a1, unit0, inverse0 = norm_forward(x0, gains[0], shifts[0])
    whole_self = spread(a1.astype(LOW))
    qkv = product(whole_self, full_qkv).astype(LOW)
    query1 = by_heads(qkv[:, :inner], count, seqs)
    key1 = by_heads(qkv[:, inner : 2 * inner], count, seqs)
    value1 = by_heads(qkv[:, 2 * inner :], count, seqs)
    mix1 = by_rows(attend(query1, key1, value1, True), count, seqs)
    x1 = x0 + collect(product_right(mix1, full_out), None)

    a2, unit1, inverse1 = norm_forward(x1, gains[1], shifts[1])
    whole_cross = spread(a2.astype(LOW))
    query2 = by_heads(product(whole_cross, full_cq).astype(LOW), count, seqs)
    text_kv = product(whole_text, full_ckv).astype(LOW)
    key2 = by_heads(text_kv[:, :inner], count, seqs)
    value2 = by_heads(text_kv[:, inner:], count, seqs)
    mix2 = by_rows(attend(query2, key2, value2, False), count, seqs)
    x2 = x1 + collect(product_right(mix2, full_cout), None)

    a3, unit2, inverse2 = norm_forward(x2, gains[2], shifts[2])
    whole_mlp = spread(a3.astype(LOW))
    hidden = product(whole_mlp, full_up)
    active_grad = product(whole_grad, full_down)
    active, pullback = jax.vjp(gelu_exact, hidden)
    active = active.astype(LOW)
    hidden_low = pullback(active_grad)[0].astype(LOW)
    h3 = collect(product_right(hidden_low, full_up), None)
    activations = (x2 + collect(product_right(active, full_down), None)).astype(LOW)

    def reduce(parts):
        joined = parts[0] if len(parts) == 1 else jnp.concatenate(parts, axis=1)
        return lax.psum_scatter(joined, "dp", scatter_dimension=0, tiled=True).astype(WIDE)

    sum_mlp = reduce(
        [
            product_left(whole_mlp, hidden_low).astype(LOW),
            product_left(whole_grad, active).astype(LOW),
        ]
    )

    e3 = cotangent.reshape(-1, width).astype(WIDE)
    change, gain2, shift2 = norm_back(unit2, inverse2, gains[2], h3)
    e2 = e3 + change
    whole_c2 = spread(e2.astype(LOW))
    d2 = by_heads(product(whole_c2, full_cout).astype(LOW), count, seqs)
    grad_q2, grad_k2, grad_v2 = attend_back(query2, key2, value2, d2, False)
    grad_q2 = by_rows(grad_q2, count, seqs)
    grad_kv2 = jnp.concatenate(
        [by_rows(grad_k2, count, seqs), by_rows(grad_v2, count, seqs)], axis=1
    )
    h2 = collect(product_right(grad_q2, full_cq), None)
    grad_text = collect(product_right(grad_kv2, full_ckv), None)
    sum_cross = reduce(
        [
            product_left(whole_cross, grad_q2).astype(LOW),
            product_left(whole_text, grad_kv2).astype(LOW),
            product_left(whole_c2, mix2).astype(LOW),
        ]
    )

    change, gain1, shift1 = norm_back(unit1, inverse1, gains[1], h2)
    e1 = e2 + change
    whole_c1 = spread(e1.astype(LOW))
    d1 = by_heads(product(whole_c1, full_out).astype(LOW), count, seqs)
    grads = attend_back(query1, key1, value1, d1, True)
    grad_qkv = jnp.concatenate([by_rows(part, count, seqs) for part in grads], axis=1)
    h1 = collect(product_right(grad_qkv, full_qkv), None)
    sum_self = reduce(
        [
            product_left(whole_self, grad_qkv).astype(LOW),
            product_left(whole_c1, mix1).astype(LOW),
        ]
    )
    change, gain0, shift0 = norm_back(unit0, inverse0, gains[0], h1)
    grad_frames = e1 + change

    norm_sums = scatter_small(jnp.stack([gain0, gain1, gain2, shift0, shift1, shift2]))

    def cut(joined, index):
        return joined[:, index * inner : (index + 1) * inner]

    return (
        activations.reshape(frames.shape),
        grad_frames.reshape(frames.shape),
        grad_text.reshape(text_states.shape),
        cut(sum_self, 0),
        cut(sum_self, 1),
        cut(sum_self, 2),
        cut(sum_self, 3).T,
        cut(sum_cross, 0),
        cut(sum_cross, 1),
        cut(sum_cross, 2),
        cut(sum_cross, 3).T,
        sum_mlp[:, :hidden_own],
        sum_mlp[:, hidden_own:].T,
        norm_sums[:3],
        norm_sums[3:],
    )


ROW, COLUMN, CORE, FAR, NEAR = 16, 8, 4, 2, 1


def exchange(value, mask):
    return lax.ppermute(value, ("dp", "tensor"), [(i, i ^ mask) for i in range(32)])


def bit(mask):
    index = lax.axis_index("dp") * 4 + lax.axis_index("tensor")
    return (index // mask) % 2 == 1


def ordered(flag, own, other, axis):
    return jnp.where(
        flag,
        jnp.concatenate([other, own], axis=axis),
        jnp.concatenate([own, other], axis=axis),
    )


def to_local_order(value):
    width = value.shape[-1] // 8
    parts = [value[..., i * width : (i + 1) * width] for i in range(8)]
    column, core = bit(COLUMN), bit(CORE)
    found = []
    for near_core in range(2):
        for near_column in range(2):
            for row in range(2):

                def pick(c, k):
                    return parts[row * 4 + (near_column ^ c) * 2 + (near_core ^ k)]

                found.append(
                    jnp.where(
                        column,
                        jnp.where(core, pick(1, 1), pick(1, 0)),
                        jnp.where(core, pick(0, 1), pick(0, 0)),
                    )
                )
    return jnp.concatenate(found, axis=-1)


def from_local_order(value):
    width = value.shape[-1] // 8
    parts = [value[..., i * width : (i + 1) * width] for i in range(8)]
    column, core = bit(COLUMN), bit(CORE)
    found = []
    for row in range(2):
        for there in range(2):
            for side in range(2):

                def pick(c, k):
                    return parts[(side ^ k) * 4 + (there ^ c) * 2 + row]

                found.append(
                    jnp.where(
                        column,
                        jnp.where(core, pick(1, 1), pick(1, 0)),
                        jnp.where(core, pick(0, 1), pick(0, 0)),
                    )
                )
    return jnp.concatenate(found, axis=-1)


def trade_rows(local):
    far = bit(FAR)
    keep = jnp.where(far, local[1], local[0])
    give = jnp.where(far, local[0], local[1])
    return jnp.concatenate([keep, exchange(give, FAR)], axis=0)


def return_rows(local, kind):
    half = local.shape[0] // 2
    other = exchange(local[half:].astype(LOW), FAR).astype(kind)
    own = local[:half].astype(kind)
    far = bit(FAR)
    return jnp.stack([jnp.where(far, other, own), jnp.where(far, own, other)])


class Line:
    def __init__(self):
        self.last = None

    def run(self, label, work, *values):
        with jax.named_scope(label):
            if self.last is not None:
                values, _ = lax.optimization_barrier((values, self.last))
            self.last = work(*values)
            return self.last


class Rows:
    def __init__(self, line, label, first, second):
        self.line, self.label, self.own = line, "rows_" + label, (first, second)
        with jax.named_scope(self.label):
            self.cross = exchange(first, ROW), exchange(second, NEAR)
            self.rest = exchange(first, NEAR), exchange(second, ROW)

    def relay(self):
        one, two = self.line.run(self.label, lambda *v: v, *self.cross)
        with jax.named_scope(self.label):
            self.cross = one, two
            self.both = exchange(one, NEAR), exchange(two, ROW)

    def finish(self):
        return self.line.run(
            self.label,
            lambda *v: jnp.concatenate(v, axis=0),
            *self.own,
            self.rest[0],
            self.cross[1],
            self.cross[0],
            self.rest[1],
            *self.both,
        )


class Sums:
    def __init__(self, line, label, work, *values):
        self.line, self.label = line, "sums_" + label

        def pieces(*v):
            low = work(*v).astype(LOW)
            half = low.shape[0] // 8
            return [low[i * half : (i + 1) * half] for i in range(8)]

        self.piece = line.run(self.label, pieces, *values)
        with jax.named_scope(self.label):
            self.relays = exchange(self.piece[6], ROW), exchange(self.piece[7], NEAR)
            self.direct = exchange(self.piece[4], ROW), exchange(self.piece[3], NEAR)

    def relay(self):
        def add(a, b, c, d):
            return (
                (a.astype(WIDE) + b.astype(WIDE)).astype(LOW),
                (c.astype(WIDE) + d.astype(WIDE)).astype(LOW),
            )

        one, two = self.line.run(
            self.label, add, self.piece[2], self.relays[0], self.piece[5], self.relays[1]
        )
        with jax.named_scope(self.label):
            self.second = exchange(one, NEAR), exchange(two, ROW)

    def finish(self, work, *more):
        def total(a, b, c, d, e, f, *v):
            first = a.astype(WIDE) + b.astype(WIDE) + c.astype(WIDE)
            second = d.astype(WIDE) + e.astype(WIDE) + f.astype(WIDE)
            return work(jnp.concatenate([first, second], axis=0), *v)

        return self.line.run(
            self.label,
            total,
            self.piece[0],
            self.direct[0],
            self.second[0],
            self.piece[1],
            self.direct[1],
            self.second[1],
            *more,
        )


class Weights:
    def __init__(self, line, label, *parts):
        self.line, self.label = line, "weights_" + label
        self.cuts = [part.shape[1] // 2 for part in parts]

        def split(*shards):
            row = bit(ROW)
            lows = jnp.concatenate([p[:, :c] for p, c in zip(shards, self.cuts)], axis=1)
            highs = jnp.concatenate([p[:, c:] for p, c in zip(shards, self.cuts)], axis=1)
            return jnp.where(row, highs, lows), jnp.where(row, lows, highs)

        self.own, give = line.run(self.label, split, *parts)
        self.send(give, ROW)

    def send(self, value, mask):
        with jax.named_scope(self.label):
            self.got = exchange(value, mask)

    def far(self):
        self.own = self.line.run(
            self.label, lambda o, g: ordered(bit(ROW), o, g, 0), self.own, self.got
        )
        self.send(self.own, FAR)

    def column(self):
        def join(own, other):
            pieces, start = [], 0
            for c in self.cuts:
                pieces += [own[:, start : start + c], other[:, start : start + c]]
                start += c
            return jnp.concatenate(pieces, axis=1)

        self.own = self.line.run(self.label, join, self.own, self.got)
        self.send(self.own, COLUMN)

    def core(self):
        self.own = self.line.run(
            self.label, lambda o, g: jnp.concatenate([o, g], axis=0), self.own, self.got
        )
        self.send(self.own, CORE)

    def finish(self):
        return self.line.run(
            self.label, lambda o, g: jnp.concatenate([o, g], axis=0), self.own, self.got
        )


class Gradients:
    def __init__(self, line, label, cuts, work, *values):
        self.line, self.label, self.cuts = line, "grads_" + label, cuts

        def halves(*v):
            pairs = work(*v)
            keep = [gradient(a[:, : a.shape[1] // 2], u).astype(LOW) for a, u in pairs]
            give = [gradient(a[:, a.shape[1] // 2 :], u).astype(LOW) for a, u in pairs]
            return (join(keep, 1), join(give, 1))

        self.own, give = line.run(self.label, halves, *values)
        self.send(give, CORE)

    def send(self, value, mask):
        with jax.named_scope(self.label):
            self.got = exchange(value, mask)

    def column(self):
        def cut(own, got):
            half = own.shape[0] // 2
            return (
                (own[:half].astype(WIDE) + got[:half].astype(WIDE)).astype(LOW),
                (own[half:].astype(WIDE) + got[half:].astype(WIDE)).astype(LOW),
            )

        self.own, give = self.line.run(self.label, cut, self.own, self.got)
        self.send(give, COLUMN)

    def far(self):
        def cut(own, got):
            total = own.astype(WIDE) + got.astype(WIDE)
            stay, leave, start = [], [], 0
            for c in self.cuts:
                stay.append(total[:, start : start + c])
                leave.append(total[:, start + c : start + 2 * c])
                start += 2 * c
            return join(stay, 1), join(leave, 1).astype(LOW)

        self.own, give = self.line.run(self.label, cut, self.own, self.got)
        self.send(give, FAR)

    def row(self):
        def cut(own, got):
            total = own + got.astype(WIDE)
            row, half = bit(ROW), own.shape[0] // 2
            return (
                jnp.where(row, total[half:], total[:half]),
                jnp.where(row, total[:half], total[half:]).astype(LOW),
            )

        self.own, give = self.line.run(self.label, cut, self.own, self.got)
        self.send(give, ROW)

    def finish(self):
        def place(own, got):
            got, row = got.astype(WIDE), bit(ROW)
            found, start = [], 0
            for c in self.cuts:
                found.append(ordered(row, own[:, start : start + c], got[:, start : start + c], 1))
                start += c
            return found

        return self.line.run(self.label, place, self.own, self.got)


def join(parts, axis):
    return parts[0] if len(parts) == 1 else jnp.concatenate(parts, axis=axis)


def gradient(operand, upstream):
    return product_left(operand, upstream)


def head_weights(queries, keys, mask):
    scores = lax.dot_general(queries, keys, (((1,), (1,)), ((), ())), preferred_element_type=WIDE)
    scores = scores * HEAD_DIM**-0.5
    if mask is not None:
        scores = jnp.where(mask, scores, -1e30)
    raw = jnp.exp(scores - jnp.max(scores, axis=-1, keepdims=True))
    return raw * (1.0 / jnp.sum(raw, axis=-1, keepdims=True))


def attend_kernel(heads, causal, q_ref, k_ref, v_ref, down_ref, along_ref, out_ref):
    mask = down_ref[...] >= along_ref[...] if causal else None
    for head in range(heads):
        columns = slice(head * HEAD_DIM, (head + 1) * HEAD_DIM)
        chance = head_weights(q_ref[:, columns], k_ref[:, columns], mask)
        mixed = jnp.dot(chance.astype(LOW), v_ref[:, columns], preferred_element_type=WIDE)
        out_ref[:, columns] = mixed.astype(LOW)


def attend_back_kernel(
    heads, causal, q_ref, k_ref, v_ref, up_ref, down_ref, along_ref, dq_ref, dk_ref, dv_ref
):
    mask = down_ref[...] >= along_ref[...] if causal else None
    scaling = HEAD_DIM**-0.5
    for head in range(heads):
        columns = slice(head * HEAD_DIM, (head + 1) * HEAD_DIM)
        queries, keys, upstream = q_ref[:, columns], k_ref[:, columns], up_ref[:, columns]
        chance = head_weights(queries, keys, mask)
        grad = lax.dot_general(
            upstream, v_ref[:, columns], (((1,), (1,)), ((), ())), preferred_element_type=WIDE
        )
        dots = jnp.sum(chance * grad, axis=-1, keepdims=True)
        score_grad = (chance * (grad - dots)).astype(LOW)
        dq_ref[:, columns] = (
            jnp.dot(score_grad, keys, preferred_element_type=WIDE) * scaling
        ).astype(LOW)
        dk_ref[:, columns] = (product_left(score_grad, queries) * scaling).astype(LOW)
        dv_ref[:, columns] = product_left(chance.astype(LOW), upstream).astype(LOW)


def column_block(rows, width, index):
    return pl.BlockSpec((rows, width), lambda s: (s, index))


def attention(queries, keys, values, places, causal):
    width = places[2]
    rows, key_rows = queries[0].shape[0] // 2, keys[0].shape[0] // 2
    heads = width // HEAD_DIM
    return pl.pallas_call(
        functools.partial(attend_kernel, heads, causal),
        grid=(2,),
        in_specs=[
            column_block(rows, width, queries[1]),
            column_block(key_rows, width, keys[1]),
            column_block(key_rows, width, values[1]),
            pl.BlockSpec(places[0].shape, lambda s: (0, 0)),
            pl.BlockSpec(places[1].shape, lambda s: (0, 0)),
        ],
        out_specs=column_block(rows, width, 0),
        out_shape=jax.ShapeDtypeStruct((2 * rows, width), LOW),
        cost_estimate=pl.CostEstimate(
            flops=8 * rows * key_rows * width, bytes_accessed=8 * rows * width * 2, transcendentals=2 * heads * rows * key_rows
        ),
        name="attend",
    )(queries[0], keys[0], values[0], places[0], places[1])


def attention_back(queries, keys, values, upstream, places, causal):
    width = places[2]
    rows, key_rows = queries[0].shape[0] // 2, keys[0].shape[0] // 2
    heads = width // HEAD_DIM
    return pl.pallas_call(
        functools.partial(attend_back_kernel, heads, causal),
        grid=(2,),
        in_specs=[
            column_block(rows, width, queries[1]),
            column_block(key_rows, width, keys[1]),
            column_block(key_rows, width, values[1]),
            column_block(rows, width, 0),
            pl.BlockSpec(places[0].shape, lambda s: (0, 0)),
            pl.BlockSpec(places[1].shape, lambda s: (0, 0)),
        ],
        out_specs=[
            column_block(rows, width, 0),
            column_block(key_rows, width, 0),
            column_block(key_rows, width, 0),
        ],
        out_shape=[
            jax.ShapeDtypeStruct((2 * rows, width), LOW),
            jax.ShapeDtypeStruct((2 * key_rows, width), LOW),
            jax.ShapeDtypeStruct((2 * key_rows, width), LOW),
        ],
        cost_estimate=pl.CostEstimate(
            flops=20 * rows * key_rows * width, bytes_accessed=14 * rows * width * 2, transcendentals=2 * heads * rows * key_rows
        ),
        name="attend_back",
    )(queries[0], keys[0], values[0], upstream, places[0], places[1])


def on_device_pairs(
    frames,
    text_states,
    self_q,
    self_k,
    self_v,
    self_out,
    cross_q,
    cross_k,
    cross_v,
    cross_out,
    mlp_up,
    mlp_down,
    norm_gains,
    norm_shifts,
    cotangent,
):
    inner, units = self_q.shape[1], mlp_up.shape[1]
    own_frames = frames.shape[1]
    line = Line()

    far_bit = bit(FAR)

    def divide(v):
        return jnp.where(far_bit, v[1], v[0]), jnp.where(far_bit, v[0], v[1])

    keep_frames, give_frames = line.run("frames", divide, frames)
    got_frames = exchange(give_frames, FAR)
    w_qkv = Weights(line, "qkv", self_q, self_k, self_v)
    w_out = Weights(line, "out", self_out.T)
    norms = line.run("norms", lambda a, b: jnp.concatenate([a, b], axis=0), norm_gains, norm_shifts)
    for axis, step in levels():
        got = swap(norms, axis, step)
        upper = (lax.axis_index(axis) // step) % 2 == 1
        norms = line.run("norms", lambda o, g: ordered(upper, o, g, 1), norms, got)
        if step == 1 and axis == "dp":
            w_qkv.far()
    norms = line.run("norms", to_local_order, norms)
    gains, shifts = norms[:3], norms[3:]

    near, far = bit(NEAR).astype(jnp.int32), bit(FAR).astype(jnp.int32)
    starts = [2 * far + near, 2 * (1 - far) + near, 2 * far + 1 - near, 2 * (1 - far) + 1 - near]
    steps = jnp.arange(own_frames, dtype=jnp.int32)
    position = jnp.concatenate([start * own_frames + steps for start in starts])
    places = (position[:, None], position[None, :], inner)

    def halves(v):
        half = v.shape[0] // 2
        return v[:half], v[half:]

    def open_rows(kept, got, gain, shift):
        x0 = to_local_order(jnp.concatenate([kept, got], axis=0)).astype(WIDE)
        a1, unit, inverse = norm_forward(x0, gain, shift)
        return (x0, unit, inverse, *halves(a1.astype(LOW)))

    x0, unit0, inverse0, *a1 = line.run(
        "norm0", open_rows, keep_frames, got_frames, gains[0], shifts[0]
    )
    rows_a1 = Rows(line, "a1", *a1)
    w_out.far()
    keep_text, give_text = line.run("text", divide, text_states)
    got_text = exchange(give_text, FAR)
    keep_grad, give_grad = line.run("cotangent", divide, cotangent)
    got_grad = exchange(give_grad, FAR)
    w_mid = Weights(line, "mid", cross_q, cross_k, cross_v, cross_out.T)
    w_up = Weights(line, "up", mlp_up)
    w_down = Weights(line, "down", mlp_down.T)
    rows_a1.relay()
    w_qkv.column()
    w_out.column()
    w_mid.far()
    whole_self = rows_a1.finish()
    w_up.far()
    w_down.far()

    def trade(kept, got):
        return halves(to_local_order(jnp.concatenate([kept, got], axis=0)))

    text_local = line.run("text", trade, keep_text, got_text)
    rows_text = Rows(line, "text", *text_local)
    grad_local = line.run("cotangent", trade, keep_grad, got_grad)
    rows_c3 = Rows(line, "c3", *grad_local)
    w_qkv.core()
    rows_text.relay()
    full_qkv = w_qkv.finish()
    w_out.core()
    rows_c3.relay()
    qkv = line.run("qkv", lambda a, w: product(a, w).astype(LOW), whole_self, full_qkv)
    full_out = w_out.finish()
    w_mid.column()
    mix1 = line.run("mix1", lambda q: attention((q, 0), (q, 1), (q, 2), places, True), qkv)
    sums_x1 = Sums(line, "x1", product_right, mix1, full_out)
    whole_text = rows_text.finish()
    whole_grad = rows_c3.finish()
    sums_x1.relay()
    w_up.column()

    def open_next(total, before, gain, shift):
        x = before + total
        a, unit, inverse = norm_forward(x, gain, shift)
        return (x, unit, inverse, *halves(a.astype(LOW)))

    x1, unit1, inverse1, *a2 = sums_x1.finish(open_next, x0, gains[1], shifts[1])
    rows_a2 = Rows(line, "a2", *a2)
    w_mid.core()
    rows_a2.relay()
    full_mid = w_mid.finish()
    full_cq = full_mid[:, :inner]
    full_ckv = full_mid[:, inner : 3 * inner]
    full_cout = full_mid[:, 3 * inner :]
    text_kv = line.run(
        "text_kv", lambda a, w: product(a, w).astype(LOW), whole_text, full_ckv
    )
    whole_cross = rows_a2.finish()
    query2 = line.run("query2", lambda a, w: product(a, w).astype(LOW), whole_cross, full_cq)
    mix2 = line.run(
        "mix2",
        lambda q, kv: attention((q, 0), (kv, 0), (kv, 1), places, False),
        query2,
        text_kv,
    )
    sums_x2 = Sums(line, "x2", product_right, mix2, full_cout)
    w_up.core()
    w_down.column()
    sums_x2.relay()
    full_up = w_up.finish()
    x2, unit2, inverse2, *a3 = sums_x2.finish(open_next, x1, gains[2], shifts[2])
    rows_a3 = Rows(line, "a3", *a3)
    w_down.core()
    rows_a3.relay()
    full_down = w_down.finish()
    active_grad = line.run("active_grad", product, whole_grad, full_down)
    whole_mlp = rows_a3.finish()

    def middle(rows, weights, upstream):
        hidden = product(rows, weights)
        active, pullback = jax.vjp(gelu_exact, hidden)
        return active.astype(LOW), pullback(upstream)[0].astype(LOW)

    active, hidden_low = line.run("hidden", middle, whole_mlp, full_up, active_grad)
    sums_h3 = Sums(line, "h3", product_right, hidden_low, full_up)
    g_up = Gradients(line, "up", [units // 2], lambda a, u: [(a, u)], whole_mlp, hidden_low)
    sums_h3.relay()
    g_up.column()
    g_down = Gradients(line, "down", [units // 2], lambda a, u: [(a, u)], whole_grad, active)

    def close_norm(total, unit, inverse, gain, before):
        change, gain_grad, shift_grad = norm_back(unit, inverse, gain, total)
        e = before + change
        return (e, gain_grad, shift_grad, *halves(e.astype(LOW)))

    e3 = jnp.concatenate(grad_local, axis=0).astype(WIDE)
    e2, gain2, shift2, *c2 = sums_h3.finish(close_norm, unit2, inverse2, gains[2], e3)
    rows_c2 = Rows(line, "c2", *c2)
    g_down.column()
    rows_c2.relay()
    sums_act = Sums(line, "act", product_right, active, full_down)
    whole_c2 = rows_c2.finish()
    d2 = line.run("d2", lambda a, w: product(a, w).astype(LOW), whole_c2, full_cout)
    grad_q2, grad_k2, grad_v2 = line.run(
        "mix2_back",
        lambda q, kv, d: attention_back((q, 0), (kv, 0), (kv, 1), d, places, False),
        query2,
        text_kv,
        d2,
    )
    sums_h2 = Sums(line, "h2", product_right, grad_q2, full_cq)
    g_up.far()
    sums_act.relay()
    g_cross = Gradients(
        line,
        "cross",
        [inner // 2] * 4,
        lambda a, q, t, k, v, c, m: [(a, q), (t, k), (t, v), (c, m)],
        whole_cross,
        grad_q2,
        whole_text,
        grad_k2,
        grad_v2,
        whole_c2,
        mix2,
    )
    sums_h2.relay()
    g_cross.column()
    sums_text = Sums(
        line,
        "text",
        lambda k, v, w: product_right(k, w[:, :inner]) + product_right(v, w[:, inner:]),
        grad_k2,
        grad_v2,
        full_ckv,
    )
    e1, gain1, shift1, *c1 = sums_h2.finish(close_norm, unit1, inverse1, gains[1], e2)
    rows_c1 = Rows(line, "c1", *c1)
    g_down.far()
    rows_c1.relay()
    g_up.row()
    sums_text.relay()
    whole_c1 = rows_c1.finish()
    d1 = line.run("d1", lambda a, w: product(a, w).astype(LOW), whole_c1, full_out)
    grads1 = line.run(
        "mix1_back",
        lambda q, d: attention_back((q, 0), (q, 1), (q, 2), d, places, True),
        qkv,
        d1,
    )
    grad_qkv = jnp.concatenate(grads1, axis=1)
    sums_h1 = Sums(line, "h1", product_right, grad_qkv, full_qkv)
    g_self = Gradients(
        line,
        "self",
        [inner // 2] * 4,
        lambda a, u, c, m: [(a, u), (c, m)],
        whole_self,
        grad_qkv,
        whole_c1,
        mix1,
    )
    sums_h1.relay()
    g_self.column()
    g_cross.far()
    g_down.row()
    e0, gain0, shift0, *_ = sums_h1.finish(close_norm, unit0, inverse0, gains[0], e1)

    def leave(local):
        local = from_local_order(local)
        half = local.shape[0] // 2
        return local[:half], local[half:].astype(LOW)

    keep_e0, give_e0 = line.run("frames", leave, e0)
    got_e0 = exchange(give_e0, FAR)
    act_local = sums_act.finish(lambda total, x: (x + total).astype(LOW), x2)
    keep_act, give_act = line.run("act", leave, act_local)
    got_act = exchange(give_act, FAR)
    text_sum = sums_text.finish(lambda total: total)
    keep_text, give_text = line.run("text", leave, text_sum)
    got_text = exchange(give_text, FAR)
    norm_sums = jnp.stack([gain0, gain1, gain2, shift0, shift1, shift2])
    norm_sums = line.run("norm_sums", from_local_order, norm_sums)
    g_self.far()
    g_cross.row()
    for axis, step in reversed(levels()):
        upper = (lax.axis_index(axis) // step) % 2 == 1
        half = norm_sums.shape[1] // 2
        give = line.run("norm_sums", lambda v: jnp.where(upper, v[:, :half], v[:, half:]), norm_sums)
        got = swap(give, axis, step)
        norm_sums = line.run(
            "norm_sums",
            lambda v, g: jnp.where(upper, v[:, half:], v[:, :half]) + g,
            norm_sums,
            got,
        )
    (grad_up,) = g_up.finish()
    (grad_down,) = g_down.finish()
    grad_cq, grad_ck, grad_cv, grad_cout = g_cross.finish()
    g_self.row()
    grad_q, grad_k, grad_v, grad_out = g_self.finish()

    def arrive(own, other):
        own, other = own, other.astype(own.dtype)
        return jnp.stack([jnp.where(far_bit, other, own), jnp.where(far_bit, own, other)])

    return (
        arrive(keep_act, got_act),
        arrive(keep_e0, got_e0),
        arrive(keep_text, got_text),
        grad_q,
        grad_k,
        grad_v,
        grad_out.T,
        grad_cq,
        grad_ck,
        grad_cv,
        grad_cout.T,
        grad_up,
        grad_down.T,
        norm_sums[:3],
        norm_sums[3:],
    )


def solution(mesh):
    rows = P("dp", "tensor", None)
    into = P("dp", "tensor")
    out_of = P("tensor", "dp")
    norms = P(None, ("dp", "tensor"))
    weights = (into, into, into, out_of, into, into, into, out_of, into, out_of)
    paired = dict(mesh.shape) == {"dp": 8, "tensor": 4}
    return jax.shard_map(
        on_device_pairs if paired else on_device,
        mesh=mesh,
        in_specs=(rows, rows, *weights, norms, norms, rows),
        out_specs=(rows, rows, rows, *weights, norms, norms),
        check_vma=False,
    )
```

```python
import functools
import math

import jax
import jax.numpy as jnp
from jax import lax
from jax.experimental import pallas as pl
from jax.experimental.pallas import tpu as pltpu
from jax.sharding import Mesh, PartitionSpec as P

HEAD_DIM = 64
EPS = 1e-05
LOW = jnp.bfloat16
WIDE = jnp.float32


def norm_forward(values, gain, shift):
    average = jnp.mean(values, axis=-1, keepdims=True)
    centered = values - average
    variance = jnp.mean(centered * centered, axis=-1, keepdims=True)
    inverse = lax.rsqrt(variance + EPS)
    unit = centered * inverse
    return unit * gain + shift, unit, inverse


def norm_back(unit, inverse, gain, upstream):
    scaled = upstream * gain
    mean_scaled = jnp.mean(scaled, axis=-1, keepdims=True)
    mean_product = jnp.mean(scaled * unit, axis=-1, keepdims=True)
    change = inverse * (scaled - mean_scaled - unit * mean_product)
    return change, jnp.sum(upstream * unit, axis=0), jnp.sum(upstream, axis=0)


def gelu_exact(values):
    return jax.nn.gelu(values, approximate=False)


def product(operand, matrix):
    return jnp.dot(operand, matrix, preferred_element_type=WIDE)


def product_left(operand, matrix):
    return lax.dot_general(operand, matrix, (((0,), (0,)), ((), ())), preferred_element_type=WIDE)


def product_right(operand, matrix):
    return lax.dot_general(operand, matrix, (((1,), (1,)), ((), ())), preferred_element_type=WIDE)


def swap(value, axis, stride):
    size = lax.axis_size(axis)
    return lax.ppermute(value, axis, [(i, i ^ stride) for i in range(size)])


def levels():
    found, stride = [], 1
    for axis in ("tensor", "dp"):
        step = 1
        while step < lax.axis_size(axis):
            found.append((axis, step))
            step *= 2
    return found


def gather_small(value):
    for axis, step in levels():
        upper = (lax.axis_index(axis) // step) % 2 == 1
        other = swap(value, axis, step)
        value = jnp.where(
            upper,
            jnp.concatenate([other, value], axis=-1),
            jnp.concatenate([value, other], axis=-1),
        )
    return value


def scatter_small(value):
    for axis, step in reversed(levels()):
        upper = (lax.axis_index(axis) // step) % 2 == 1
        half = value.shape[-1] // 2
        low, high = value[..., :half], value[..., half:]
        other = swap(jnp.where(upper, low, high), axis, step)
        value = jnp.where(upper, high, low) + other
    return value


def spread(local):
    gathered = lax.all_gather(local, "tensor", axis=0, tiled=False)
    return gathered.reshape(-1, local.shape[-1])


def collect(partial, shape):
    summed = lax.psum_scatter(
        partial.astype(LOW), "tensor", scatter_dimension=0, tiled=True
    )
    return summed.astype(WIDE)


def by_heads(rows, count, seqs):
    frames = rows.shape[0] // (count * seqs)
    split = rows.reshape(count, seqs, frames, -1, HEAD_DIM)
    return split.transpose(1, 3, 0, 2, 4).reshape(seqs, -1, count * frames, HEAD_DIM)


def by_rows(heads, count, seqs):
    frames = heads.shape[2] // count
    split = heads.reshape(seqs, heads.shape[1], count, frames, HEAD_DIM)
    return split.transpose(2, 0, 3, 1, 4).reshape(count * seqs * frames, -1)


def weights_of(queries, keys, causal):
    scores = jnp.einsum("shqd,shkd->shqk", queries, keys, preferred_element_type=WIDE)
    scores = scores * HEAD_DIM**-0.5
    if causal:
        length = queries.shape[2]
        visible = jnp.arange(length)[:, None] >= jnp.arange(length)[None, :]
        scores = jnp.where(visible, scores, -1e30)
    largest = jnp.max(scores, axis=-1, keepdims=True)
    raw = jnp.exp(scores - largest)
    return raw / jnp.sum(raw, axis=-1, keepdims=True)


def attend(queries, keys, values, causal):
    chance = weights_of(queries, keys, causal).astype(LOW)
    return jnp.einsum("shqk,shkd->shqd", chance, values, preferred_element_type=WIDE).astype(LOW)


def attend_back(queries, keys, values, upstream, causal):
    chance = weights_of(queries, keys, causal)
    grad = jnp.einsum("shqd,shkd->shqk", upstream, values, preferred_element_type=WIDE)
    dots = jnp.sum(chance * grad, axis=-1, keepdims=True)
    score_grad = (chance * (grad - dots)).astype(LOW)
    scaling = HEAD_DIM**-0.5
    grad_q = jnp.einsum("shqk,shkd->shqd", score_grad, keys, preferred_element_type=WIDE)
    grad_k = jnp.einsum("shqk,shqd->shkd", score_grad, queries, preferred_element_type=WIDE)
    grad_v = jnp.einsum("shqk,shqd->shkd", chance.astype(LOW), upstream, preferred_element_type=WIDE)
    return (grad_q * scaling).astype(LOW), (grad_k * scaling).astype(LOW), grad_v.astype(LOW)


def on_device(
    frames,
    text_states,
    self_q,
    self_k,
    self_v,
    self_out,
    cross_q,
    cross_k,
    cross_v,
    cross_out,
    mlp_up,
    mlp_down,
    norm_gains,
    norm_shifts,
    cotangent,
):
    seqs, own, width = frames.shape
    text_own = text_states.shape[1]
    count = lax.axis_size("tensor")
    inner = self_q.shape[1]

    norms = gather_small(jnp.concatenate([norm_gains, norm_shifts], axis=0))
    gains, shifts = norms[:3], norms[3:]

    whole_grad = spread(cotangent.reshape(-1, width))
    whole_text = spread(text_states.reshape(-1, width))

    def gather(parts):
        joined = parts[0] if len(parts) == 1 else jnp.concatenate(parts, axis=1)
        return lax.all_gather(joined, "dp", axis=0, tiled=True)

    full_qkv = gather([self_q, self_k, self_v])
    full_mid = gather([self_out.T, cross_q, cross_k, cross_v, cross_out.T])
    full_mlp = gather([mlp_up, mlp_down.T])
    full_out = full_mid[:, :inner]
    full_cq = full_mid[:, inner : 2 * inner]
    full_ckv = full_mid[:, 2 * inner : 4 * inner]
    full_cout = full_mid[:, 4 * inner :]
    hidden_own = mlp_up.shape[1]
    full_up, full_down = full_mlp[:, :hidden_own], full_mlp[:, hidden_own:]

    x0 = frames.reshape(-1, width).astype(WIDE)
    a1, unit0, inverse0 = norm_forward(x0, gains[0], shifts[0])
    whole_self = spread(a1.astype(LOW))
    qkv = product(whole_self, full_qkv).astype(LOW)
    query1 = by_heads(qkv[:, :inner], count, seqs)
    key1 = by_heads(qkv[:, inner : 2 * inner], count, seqs)
    value1 = by_heads(qkv[:, 2 * inner :], count, seqs)
    mix1 = by_rows(attend(query1, key1, value1, True), count, seqs)
    x1 = x0 + collect(product_right(mix1, full_out), None)

    a2, unit1, inverse1 = norm_forward(x1, gains[1], shifts[1])
    whole_cross = spread(a2.astype(LOW))
    query2 = by_heads(product(whole_cross, full_cq).astype(LOW), count, seqs)
    text_kv = product(whole_text, full_ckv).astype(LOW)
    key2 = by_heads(text_kv[:, :inner], count, seqs)
    value2 = by_heads(text_kv[:, inner:], count, seqs)
    mix2 = by_rows(attend(query2, key2, value2, False), count, seqs)
    x2 = x1 + collect(product_right(mix2, full_cout), None)

    a3, unit2, inverse2 = norm_forward(x2, gains[2], shifts[2])
    whole_mlp = spread(a3.astype(LOW))
    hidden = product(whole_mlp, full_up)
    active_grad = product(whole_grad, full_down)
    active, pullback = jax.vjp(gelu_exact, hidden)
    active = active.astype(LOW)
    hidden_low = pullback(active_grad)[0].astype(LOW)
    h3 = collect(product_right(hidden_low, full_up), None)
    activations = (x2 + collect(product_right(active, full_down), None)).astype(LOW)

    def reduce(parts):
        joined = parts[0] if len(parts) == 1 else jnp.concatenate(parts, axis=1)
        return lax.psum_scatter(joined, "dp", scatter_dimension=0, tiled=True).astype(WIDE)

    sum_mlp = reduce(
        [
            product_left(whole_mlp, hidden_low).astype(LOW),
            product_left(whole_grad, active).astype(LOW),
        ]
    )

    e3 = cotangent.reshape(-1, width).astype(WIDE)
    change, gain2, shift2 = norm_back(unit2, inverse2, gains[2], h3)
    e2 = e3 + change
    whole_c2 = spread(e2.astype(LOW))
    d2 = by_heads(product(whole_c2, full_cout).astype(LOW), count, seqs)
    grad_q2, grad_k2, grad_v2 = attend_back(query2, key2, value2, d2, False)
    grad_q2 = by_rows(grad_q2, count, seqs)
    grad_kv2 = jnp.concatenate(
        [by_rows(grad_k2, count, seqs), by_rows(grad_v2, count, seqs)], axis=1
    )
    h2 = collect(product_right(grad_q2, full_cq), None)
    grad_text = collect(product_right(grad_kv2, full_ckv), None)
    sum_cross = reduce(
        [
            product_left(whole_cross, grad_q2).astype(LOW),
            product_left(whole_text, grad_kv2).astype(LOW),
            product_left(whole_c2, mix2).astype(LOW),
        ]
    )

    change, gain1, shift1 = norm_back(unit1, inverse1, gains[1], h2)
    e1 = e2 + change
    whole_c1 = spread(e1.astype(LOW))
    d1 = by_heads(product(whole_c1, full_out).astype(LOW), count, seqs)
    grads = attend_back(query1, key1, value1, d1, True)
    grad_qkv = jnp.concatenate([by_rows(part, count, seqs) for part in grads], axis=1)
    h1 = collect(product_right(grad_qkv, full_qkv), None)
    sum_self = reduce(
        [
            product_left(whole_self, grad_qkv).astype(LOW),
            product_left(whole_c1, mix1).astype(LOW),
        ]
    )
    change, gain0, shift0 = norm_back(unit0, inverse0, gains[0], h1)
    grad_frames = e1 + change

    norm_sums = scatter_small(jnp.stack([gain0, gain1, gain2, shift0, shift1, shift2]))

    def cut(joined, index):
        return joined[:, index * inner : (index + 1) * inner]

    return (
        activations.reshape(frames.shape),
        grad_frames.reshape(frames.shape),
        grad_text.reshape(text_states.shape),
        cut(sum_self, 0),
        cut(sum_self, 1),
        cut(sum_self, 2),
        cut(sum_self, 3).T,
        cut(sum_cross, 0),
        cut(sum_cross, 1),
        cut(sum_cross, 2),
        cut(sum_cross, 3).T,
        sum_mlp[:, :hidden_own],
        sum_mlp[:, hidden_own:].T,
        norm_sums[:3],
        norm_sums[3:],
    )


def exchange(value, axis):
    return lax.ppermute(value, axis, [(0, 1), (1, 0)])


def bit(axis):
    return lax.axis_index(axis) == 1


def ordered(flag, own, other, axis):
    return jnp.where(
        flag,
        jnp.concatenate([other, own], axis=axis),
        jnp.concatenate([own, other], axis=axis),
    )


def regroup(value, outer):
    width, inner = value.shape[-1] // 8, 8 // outer
    parts = [value[..., i * width : (i + 1) * width] for i in range(8)]
    order = [parts[o * inner + i] for i in range(inner) for o in range(outer)]
    return jnp.concatenate(order, axis=-1)


def halves(v):
    half = v.shape[0] // 2
    return v[:half], v[half:]


def join(parts, axis):
    return parts[0] if len(parts) == 1 else jnp.concatenate(parts, axis=axis)


VMEM_BYTES = 40 << 20


def whole_block(shape):
    return pl.BlockSpec(shape, lambda *i: (0,) * len(shape), pipeline_mode=pl.Buffered(1))


def settings():
    return dict(
        cost_estimate=pl.CostEstimate(flops=1, bytes_accessed=1, transcendentals=0),
        compiler_params=pltpu.CompilerParams(vmem_limit_bytes=VMEM_BYTES),
    )


def fill(pieces, whole_ref):
    start = 0
    for piece in pieces:
        whole_ref[start : start + piece.shape[0], :] = piece[...]
        start += piece.shape[0]


def rows_product(pieces, weights, first, count, tile):
    depth = weights.shape[0]
    rows = sum(p.shape[0] for p in pieces)

    def body(*refs):
        w_ref, whole_ref, out_ref = refs[len(pieces) :]

        @pl.when(pl.program_id(0) == 0)
        def _():
            fill(refs[: len(pieces)], whole_ref)

        out_ref[...] = jnp.dot(
            whole_ref[...], w_ref[...], preferred_element_type=WIDE
        ).astype(LOW)

    return pl.pallas_call(
        body,
        grid=(count // tile,),
        in_specs=[whole_block(p.shape) for p in pieces]
        + [pl.BlockSpec((depth, tile), lambda j: (0, first + j))],
        out_specs=[
            pl.BlockSpec((rows, depth), lambda j: (0, 0)),
            pl.BlockSpec((rows, tile), lambda j: (0, j)),
        ],
        out_shape=[
            jax.ShapeDtypeStruct((rows, depth), LOW),
            jax.ShapeDtypeStruct((rows, count), LOW),
        ],
        name="rows_product",
        **settings(),
    )(*pieces, weights)


def middle_kernel(*refs):
    pieces, (up_ref, down_ref, grad_ref, whole_ref, active_ref, low_ref) = refs[:7], refs[7:]

    @pl.when(pl.program_id(0) == 0)
    def _():
        fill(line_pieces([piece[...] for piece in pieces]), whole_ref)

    hidden = jnp.dot(whole_ref[...], up_ref[...], preferred_element_type=WIDE)
    upstream = jnp.dot(grad_ref[...], down_ref[...], preferred_element_type=WIDE)
    share = 0.5 + 0.5 * lax.erf(hidden * 0.5**0.5)
    density = jnp.exp(-0.5 * hidden * hidden) * (2.0 * math.pi) ** -0.5
    active_ref[...] = (hidden * share).astype(LOW)
    low_ref[...] = (upstream * (share + hidden * density)).astype(LOW)


def middle(pieces, weights, grad, tile):
    depth, count = weights.shape[0], weights.shape[1] // 2
    rows = grad.shape[0]
    tiles = count // tile
    out = pl.BlockSpec((rows, tile), lambda j: (0, j))
    return pl.pallas_call(
        middle_kernel,
        grid=(tiles,),
        in_specs=[whole_block(p.shape) for p in pieces]
        + [
            pl.BlockSpec((depth, tile), lambda j: (0, j)),
            pl.BlockSpec((depth, tile), lambda j: (0, tiles + j)),
            whole_block(grad.shape),
        ],
        out_specs=[pl.BlockSpec((rows, depth), lambda j: (0, 0)), out, out],
        out_shape=[jax.ShapeDtypeStruct((rows, n), LOW) for n in (depth, count, count)],
        name="middle",
        **settings(),
    )(*pieces, weights, weights, grad)


def pieces_product(terms, tile, cuts=(2, 2, 2, 1, 1)):
    rows, depth = terms[0][0].shape[0], terms[0][1].shape[0]
    unit = rows // sum(cuts)

    def body(*refs):
        total = None
        for i in range(len(terms)):
            term = lax.dot_general(
                refs[2 * i][...],
                refs[2 * i + 1][...],
                (((1,), (1,)), ((), ())),
                preferred_element_type=WIDE,
            )
            total = term if total is None else total + term
        fill_from = 0
        for ref in refs[2 * len(terms) :]:
            ref[...] = total[fill_from : fill_from + ref.shape[0]].astype(LOW)
            fill_from += ref.shape[0]

    specs, operands = [], []
    for x, w, block in terms:
        specs.append(whole_block(x.shape))
        specs.append(pl.BlockSpec((tile, x.shape[1]), lambda i, block=block: (i, block)))
        operands += [x, w]
    sizes = [unit * cut for cut in cuts]
    return pl.pallas_call(
        body,
        grid=(depth // tile,),
        in_specs=specs,
        out_specs=[pl.BlockSpec((n, tile), lambda i: (0, i)) for n in sizes],
        out_shape=[jax.ShapeDtypeStruct((n, depth), LOW) for n in sizes],
        name="pieces_product",
        **settings(),
    )(*operands)


def gradient_product(pairs, tile):
    depth = pairs[0][0].shape[1]
    tiles = [u.shape[1] // tile for _, u in pairs]
    starts = [sum(tiles[:i]) for i in range(len(tiles))]

    def body(*refs):
        out_ref, j = refs[-1], pl.program_id(0)
        for i in range(len(pairs)):

            @pl.when((j >= starts[i]) & (j < starts[i] + tiles[i]))
            def _(i=i):
                out_ref[...] = product_left(refs[2 * i][...], refs[2 * i + 1][...]).astype(LOW)

    specs, operands = [], []
    for (a, u), start, count in zip(pairs, starts, tiles):
        specs.append(whole_block(a.shape))
        specs.append(
            pl.BlockSpec(
                (u.shape[0], tile),
                lambda j, start=start, count=count: (0, jnp.clip(j - start, 0, count - 1)),
            )
        )
        operands += [a, u]
    return pl.pallas_call(
        body,
        grid=(sum(tiles),),
        in_specs=specs,
        out_specs=pl.BlockSpec((depth, tile), lambda j: (0, j)),
        out_shape=jax.ShapeDtypeStruct((depth, tile * sum(tiles)), LOW),
        name="gradient_product",
        **settings(),
    )(*operands)


def relay_kernel(near_ref, row_ref, one_ref, two_ref, near_out, row_out):
    half = one_ref.shape[0]
    near_out[:half] = (near_ref[:half].astype(WIDE) + one_ref[...].astype(WIDE)).astype(LOW)
    near_out[half:] = near_ref[half:]
    row_out[:half] = row_ref[:half]
    row_out[half:] = (row_ref[half:].astype(WIDE) + two_ref[...].astype(WIDE)).astype(LOW)


def relay_sums(near, row, one, two):
    return pl.pallas_call(
        relay_kernel,
        out_shape=[jax.ShapeDtypeStruct(near.shape, LOW)] * 2,
        name="relay_sums",
        **settings(),
    )(near, row, one, two)


def open_kernel(own_ref, near_ref, row_ref, x_ref, gain_ref, shift_ref, x_out, a_out):
    total = own_ref[...].astype(WIDE) + near_ref[...].astype(WIDE) + row_ref[...].astype(WIDE)
    x = x_ref[...] + total
    x_out[...] = x
    a_out[...] = norm_forward(x, gain_ref[...], shift_ref[...])[0].astype(LOW)


def open_norm(own, near, row, x, gain, shift):
    return pl.pallas_call(
        open_kernel,
        out_shape=[jax.ShapeDtypeStruct(x.shape, WIDE), jax.ShapeDtypeStruct(x.shape, LOW)],
        name="open_norm",
        **settings(),
    )(own, near, row, x, gain, shift)


def close_kernel(own_ref, near_ref, row_ref, x_ref, gain_ref, e_ref, e_out, c_out, sums_out):
    total = own_ref[...].astype(WIDE) + near_ref[...].astype(WIDE) + row_ref[...].astype(WIDE)
    _, unit, inverse = norm_forward(x_ref[...], gain_ref[...], 0.0)
    change, gain_grad, shift_grad = norm_back(unit, inverse, gain_ref[...], total)
    e = e_ref[...].astype(WIDE) + change
    e_out[...] = e
    c_out[...] = e.astype(LOW)
    sums_out[...] = jnp.concatenate([gain_grad[None], shift_grad[None]], axis=0)


def close_norm(own, near, row, x, gain, e):
    return pl.pallas_call(
        close_kernel,
        out_shape=[
            jax.ShapeDtypeStruct(x.shape, WIDE),
            jax.ShapeDtypeStruct(x.shape, LOW),
            jax.ShapeDtypeStruct((2, x.shape[1]), WIDE),
        ],
        name="close_norm",
        **settings(),
    )(own, near, row, x, gain, e)


def plain_total(a, b, c):
    return a.astype(WIDE) + b.astype(WIDE) + c.astype(WIDE)


def head_weights(queries, keys, mask):
    scores = lax.dot_general(queries, keys, (((1,), (1,)), ((), ())), preferred_element_type=WIDE)
    scores = scores * HEAD_DIM**-0.5
    if mask is not None:
        scores = jnp.where(mask, scores, -1e30)
    raw = jnp.exp(scores - jnp.max(scores, axis=-1, keepdims=True))
    return raw * (1.0 / jnp.sum(raw, axis=-1, keepdims=True))


def attend_kernel(heads, causal, q_ref, k_ref, v_ref, down_ref, along_ref, out_ref):
    mask = down_ref[...] >= along_ref[...] if causal else None
    for head in range(heads):
        columns = slice(head * HEAD_DIM, (head + 1) * HEAD_DIM)
        chance = head_weights(q_ref[:, columns], k_ref[:, columns], mask)
        mixed = jnp.dot(chance.astype(LOW), v_ref[:, columns], preferred_element_type=WIDE)
        out_ref[:, columns] = mixed.astype(LOW)


def attend_back_kernel(
    heads, causal, q_ref, k_ref, v_ref, up_ref, down_ref, along_ref, dq_ref, dk_ref, dv_ref
):
    mask = down_ref[...] >= along_ref[...] if causal else None
    scaling = HEAD_DIM**-0.5
    for head in range(heads):
        columns = slice(head * HEAD_DIM, (head + 1) * HEAD_DIM)
        queries, keys, upstream = q_ref[:, columns], k_ref[:, columns], up_ref[:, columns]
        chance = head_weights(queries, keys, mask)
        grad = lax.dot_general(
            upstream, v_ref[:, columns], (((1,), (1,)), ((), ())), preferred_element_type=WIDE
        )
        dots = jnp.sum(chance * grad, axis=-1, keepdims=True)
        score_grad = (chance * (grad - dots)).astype(LOW)
        dq_ref[:, columns] = (
            jnp.dot(score_grad, keys, preferred_element_type=WIDE) * scaling
        ).astype(LOW)
        dk_ref[:, columns] = (product_left(score_grad, queries) * scaling).astype(LOW)
        dv_ref[:, columns] = product_left(chance.astype(LOW), upstream).astype(LOW)


def column_block(rows, width, index):
    return pl.BlockSpec((rows, width), lambda s: (s, index))


def attention(queries, keys, values, places, causal):
    width = places[2]
    rows, key_rows = queries[0].shape[0] // 2, keys[0].shape[0] // 2
    heads = width // HEAD_DIM
    return pl.pallas_call(
        functools.partial(attend_kernel, heads, causal),
        grid=(2,),
        in_specs=[
            column_block(rows, width, queries[1]),
            column_block(key_rows, width, keys[1]),
            column_block(key_rows, width, values[1]),
            pl.BlockSpec(places[0].shape, lambda s: (0, 0)),
            pl.BlockSpec(places[1].shape, lambda s: (0, 0)),
        ],
        out_specs=column_block(rows, width, 0),
        out_shape=jax.ShapeDtypeStruct((2 * rows, width), LOW),
        **settings(),
        name="attend",
    )(queries[0], keys[0], values[0], places[0], places[1])


def attention_back(queries, keys, values, upstream, places, causal):
    width = places[2]
    rows, key_rows = queries[0].shape[0] // 2, keys[0].shape[0] // 2
    heads = width // HEAD_DIM
    return pl.pallas_call(
        functools.partial(attend_back_kernel, heads, causal),
        grid=(2,),
        in_specs=[
            column_block(rows, width, queries[1]),
            column_block(key_rows, width, keys[1]),
            column_block(key_rows, width, values[1]),
            column_block(rows, width, 0),
            pl.BlockSpec(places[0].shape, lambda s: (0, 0)),
            pl.BlockSpec(places[1].shape, lambda s: (0, 0)),
        ],
        out_specs=[
            column_block(rows, width, 0),
            column_block(key_rows, width, 0),
            column_block(key_rows, width, 0),
        ],
        out_shape=[
            jax.ShapeDtypeStruct((2 * rows, width), LOW),
            jax.ShapeDtypeStruct((2 * key_rows, width), LOW),
            jax.ShapeDtypeStruct((2 * key_rows, width), LOW),
        ],
        **settings(),
        name="attend_back",
    )(queries[0], keys[0], values[0], upstream, places[0], places[1])


def line_pieces(pieces):
    local, d1, u3, d2, u2, u1, d3 = pieces
    return local, d1 + u3, d2 + u2, u1 + d3


class Name:
    def __getattr__(self, key):
        return self.__dict__.setdefault(key, Name())


def swapping(axis):
    return lambda v: exchange(v, axis)


def stepping(*perm):
    return lambda v: lax.ppermute(v, ("far", "near"), perm)


to_row, to_column, to_core = swapping("row"), swapping("column"), swapping("core")
to_far, to_near = swapping("far"), swapping("near")
up_all, up_last2, up_last = stepping((0, 1), (1, 2), (2, 3)), stepping((1, 2), (2, 3)), stepping((2, 3))
up_first, up_first2 = stepping((0, 1)), stepping((0, 1), (1, 2))
down_all, down_last2, down_last = (
    stepping((3, 2), (2, 1), (1, 0)),
    stepping((2, 1), (1, 0)),
    stepping((1, 0)),
)
down_first, down_first2 = stepping((3, 2)), stepping((3, 2), (2, 1))


def to_all(v):
    return lax.all_gather(v, ("column", "core"), axis=0, tiled=True)


def to_sum(v):
    return lax.psum_scatter(v, ("column", "core"), scatter_dimension=0, tiled=True)


def run_steps(values, order):
    last = None
    for needs, gives, work, *sends in order:
        taken = [values[n] for n in needs]
        if last is not None:
            taken, _ = lax.optimization_barrier((taken, last))
        last = work(*taken)
        values.update(zip(gives, last, strict=True))
        for result, source, move in sends:
            values[result] = move(values[source])
    return values


def keep(*values):
    return values


def row_sends(local):
    return (local.row, local, to_row), (local.near, local, to_near)


def rows_steps(local, work, needs, gives):
    def relay(row, near):
        return halves(row)[0], halves(near)[1]

    return (
        (
            (local.row, local.near),
            (local.p, local.q),
            relay,
            (local.one, local.p, to_near),
            (local.two, local.q, to_row),
        ),
        ((local.one, local.two), (local.three, local.four), keep),
        (
            (local, local.near, local.row, local.three, local.four, *needs),
            gives,
            lambda *v: work(v[:5], *v[5:]),
        ),
    )


def line_sends(local):
    return (local.u1, local, up_all), (local.d1, local, down_all)


def line_rows_steps(local, work, needs, gives):
    c = local
    return (
        ((c.u1, c.d1), (c.v1, c.w1), keep, (c.u2, c.v1, up_last2), (c.d2, c.w1, down_last2)),
        ((c.u2, c.d2), (c.v2, c.w2), keep, (c.u3, c.v2, up_last), (c.d3, c.w2, down_last)),
        ((c.u3, c.d3), (c.v3, c.w3), keep),
        (
            (c, c.w1, c.v3, c.w2, c.v2, c.v1, c.w3, *needs),
            gives,
            lambda *u: work(u[:7], *u[7:]),
        ),
    )


def line_sums_steps(terms, weights, blocks, work, needs, gives, *sends):
    count, c = len(terms), Name()

    def start(*v):
        return pieces_product(list(zip(v[:count], v[count:], blocks)), 384, (1, 1, 1, 1))

    def add(a, b, c, d):
        return (
            (a.astype(WIDE) + b.astype(WIDE)).astype(LOW),
            (c.astype(WIDE) + d.astype(WIDE)).astype(LOW),
        )

    return (
        ((*terms, *weights), (c.q0, c.q1, c.q2, c.q3), start),
        (
            (c.q0, c.q1, c.q2, c.q3),
            (c.p0, c.p1, c.p2, c.p3),
            keep,
            (c.d3, c.p1, down_first),
            (c.u3, c.p3, up_first),
        ),
        (
            (c.p2, c.d3, c.p2, c.u3),
            (c.a2, c.b2),
            add,
            (c.d2, c.a2, down_first2),
            (c.u2, c.b2, up_first2),
        ),
        (
            (c.p3, c.d2, c.p1, c.u2),
            (c.a1, c.b1),
            add,
            (c.d1, c.a1, down_all),
            (c.u1, c.b1, up_all),
        ),
        ((c.p0, c.d1, c.u1, *needs), gives, work, *sends),
    )


def sums_steps(terms, weights, blocks, work, needs, gives, *sends):
    count, c = len(terms), Name()

    def start(*v):
        return pieces_product(list(zip(v[:count], v[count:], blocks)), 384)

    return (
        (
            (*terms, *weights),
            (c.own, c.n, c.r, c.one, c.two),
            start,
            (c.a, c.one, to_row),
            (c.b, c.two, to_near),
        ),
        (
            (c.n, c.r, c.a, c.b),
            (c.c, c.d),
            relay_sums,
            (c.x, c.c, to_near),
            (c.y, c.d, to_row),
        ),
        ((c.own, c.x, c.y, *needs), gives, work, *sends),
    )


def weights_steps(parts, cuts, full):
    c = Name()

    def split(*shards):
        row = bit("row")
        lows = join([p[:, :w] for p, w in zip(shards, cuts)], 1)
        highs = join([p[:, w:] for p, w in zip(shards, cuts)], 1)
        return jnp.where(row, highs, lows), jnp.where(row, lows, highs)

    def stack(own, got):
        return (ordered(bit("row"), own, got, 0),)

    def side_by_side(own, other):
        pieces, start = [], 0
        for w in cuts:
            pieces += [own[:, start : start + w], other[:, start : start + w]]
            start += w
        return (jnp.concatenate(pieces, axis=1),)

    return (
        (parts, (c.a, c.b), split, (c.c, c.b, to_row)),
        ((c.a, c.c), (c.d,), stack, (c.e, c.d, to_far)),
        ((c.d, c.e), (c.f,), side_by_side, (full, c.f, to_all)),
    )


def gradients_steps(pairs, cuts, gives):
    n = Name()

    def make(*v):
        return (gradient_product(list(zip(v[::2], v[1::2])), 384),)

    def cut_far(total):
        stay, leave, start = [], [], 0
        for c in cuts:
            stay.append(total[:, start : start + c])
            leave.append(total[:, start + c : start + 2 * c])
            start += 2 * c
        return join(stay, 1), join(leave, 1)

    def cut_row(own, got):
        total, row = own.astype(WIDE) + got.astype(WIDE), bit("row")
        first, second = halves(total)
        return jnp.where(row, second, first), jnp.where(row, first, second).astype(LOW)

    def place(own, got):
        got, row = got.astype(WIDE), bit("row")
        found, start = [], 0
        for c in cuts:
            found.append(ordered(row, own[:, start : start + c], got[:, start : start + c], 1))
            start += c
        return found

    return (
        (pairs, (n.a,), make, (n.b, n.a, to_sum)),
        ((n.b,), (n.c, n.d), cut_far, (n.e, n.d, to_far)),
        ((n.c, n.e), (n.f, n.g), cut_row, (n.h, n.g, to_row)),
        ((n.f, n.h), gives, place),
    )


def plan_pairs(n, inner, units, own_frames, own_text):
    s, far_bit = Name(), bit("far")

    def divide(v):
        return jnp.where(far_bit, v[1], v[0]), jnp.where(far_bit, v[0], v[1])

    half, wide = inner // 2, units // 2
    s.frames = ((n.frames,), (n.keep_f, n.give_f), divide, (n.got_f, n.give_f, to_far))
    s.frames_in = ((n.got_f,), (n.got_f2,), keep)
    s.w_self, s.w_self_far, s.w_self_all = weights_steps(
        (n.self_q, n.self_k, n.self_v, n.self_out), [half] * 4, n.full_self
    )
    s.w_cross, s.w_cross_far, s.w_cross_all = weights_steps(
        (n.cross_q, n.cross_k, n.cross_v, n.cross_out), [half] * 4, n.full_cross
    )
    s.w_mlp = (
        (n.mlp_up, n.mlp_down),
        (n.own_mlp,),
        lambda a, b: (jnp.concatenate([a, b], axis=1),),
        (n.got_mlp, n.own_mlp, to_row),
    )
    s.w_mlp_all = (
        (n.own_mlp, n.got_mlp),
        (n.both_mlp,),
        lambda a, b: (ordered(bit("row"), a, b, 0),),
    )
    s.w_mlp_go = ((n.both_mlp,), (n.both_mlp2,), keep, (n.full_mlp, n.both_mlp2, to_all))

    axes, moves = ("near", "far", "core", "column", "row"), (to_near, to_far, to_core, to_column, to_row)

    def widen(axis):
        return lambda o, g: (ordered(bit(axis), o, g, 1),)

    s.n0 = (
        (n.norm_gains, n.norm_shifts),
        (n.v0,),
        lambda a, b: (jnp.concatenate([a, b], axis=0),),
        (n.g0, n.v0, moves[0]),
    )
    s.n1 = ((n.v0, n.g0), (n.v1,), widen(axes[0]), (n.g1, n.v1, moves[1]))
    s.n2 = ((n.v1, n.g1), (n.v2,), widen(axes[1]), (n.g2, n.v2, moves[2]))
    s.n3 = ((n.v2, n.g2), (n.v3,), widen(axes[2]), (n.g3, n.v3, moves[3]))
    s.n4 = ((n.v3, n.g3), (n.v4,), widen(axes[3]), (n.g4, n.v4, moves[4]))

    def open_rows(kept, got, v, g):
        norms = regroup(ordered(bit("row"), v, g, 1), 2)
        x0 = regroup(jnp.concatenate([kept, got], axis=0), 2).astype(WIDE)
        found = [norms[i : i + 1] for i in range(6)]
        return x0, norm_forward(x0, found[0], found[3])[0].astype(LOW), *found

    s.norm0 = (
        (n.keep_f, n.got_f2, n.v4, n.g4),
        (n.x0, n.a1, n.gain0, n.gain1, n.gain2, n.shift0, n.shift1, n.shift2),
        open_rows,
        *row_sends(n.a1),
    )

    near, far = lax.axis_index("near"), lax.axis_index("far")
    starts = [2 * far + near, 2 * (1 - far) + near, 2 * far + 1 - near, 2 * (1 - far) + 1 - near]
    steps = jnp.arange(own_frames, dtype=jnp.int32)
    position = jnp.concatenate([start * own_frames + steps for start in starts])
    places = (position[:, None], position[None, :], inner)

    def part_ways(t, c):
        return [jnp.concatenate(v, axis=0) for v in zip(divide(t), divide(c))]

    def trade(kept, got):
        text = jnp.concatenate([kept[:own_text], got[:own_text]], axis=0)
        grad = jnp.concatenate([kept[own_text:], got[own_text:]], axis=0)
        return regroup(text, 2), regroup(grad, 2)

    def gathered(pieces):
        return (jnp.concatenate(pieces, axis=0),)

    s.trade = (
        (n.text_states, n.cotangent),
        (n.keep_b, n.give_b),
        part_ways,
        (n.got_b, n.give_b, to_far),
    )
    s.both = ((n.keep_b, n.got_b), (n.text0, n.c3), trade, *line_sends(n.c3))
    s.text_go = ((n.text0,), (n.text,), keep, *row_sends(n.text))
    s.text_on, s.text_in, s.text_all = rows_steps(n.text, gathered, (), (n.whole_text,))
    s.c3_on, s.c3_on2, s.c3_in, s.c3_all = line_rows_steps(
        n.c3, lambda p: gathered(line_pieces(p)), (), (n.whole_grad,)
    )

    def product_of(first, count):
        return lambda p, w: rows_product(p, w, first, count * inner, inner)

    s.a1_on, s.a1_in, s.qkv = rows_steps(
        n.a1, product_of(0, 3), (n.full_self,), (n.whole_self, n.qkv)
    )
    s.mix1 = (
        (n.qkv,),
        (n.mix1,),
        lambda q: (attention((q, 0), (q, 1), (q, 2), places, True),),
    )
    s.x1, s.x1_on, s.x1_end = sums_steps(
        (n.mix1,),
        (n.full_self,),
        (3,),
        open_norm,
        (n.x0, n.gain1, n.shift1),
        (n.x1, n.a2),
        *row_sends(n.a2),
    )
    s.a2_on, s.a2_in, s.query2 = rows_steps(
        n.a2, product_of(0, 1), (n.full_cross,), (n.whole_cross, n.query2)
    )
    s.text_kv = (
        (n.whole_text, n.full_cross),
        (n.text_kv,),
        lambda a, w: rows_product([a], w, 1, 2 * inner, inner)[1:],
    )
    s.mix2 = (
        (n.query2, n.text_kv),
        (n.mix2,),
        lambda q, kv: (attention((q, 0), (kv, 0), (kv, 1), places, False),),
    )
    s.x2, s.x2_on, s.x2_end = sums_steps(
        (n.mix2,),
        (n.full_cross,),
        (3,),
        open_norm,
        (n.x1, n.gain2, n.shift2),
        (n.x2, n.a3),
        *line_sends(n.a3),
    )
    s.a3_on, s.a3_on2, s.a3_in, s.middle = line_rows_steps(
        n.a3,
        lambda p, w, g: middle(p, w, g, inner),
        (n.full_mlp, n.whole_grad),
        (n.whole_mlp, n.active, n.hidden_low),
    )
    s.h3, s.h3_go, s.h3_on, s.h3_on2, s.h3_end = line_sums_steps(
        (n.hidden_low,),
        (n.full_mlp,),
        (0,),
        close_norm,
        (n.x2, n.gain2, n.c3),
        (n.e2, n.c2, n.norm2),
        *row_sends(n.c2),
    )
    s.g_mlp = (
        (n.whole_mlp, n.hidden_low, n.whole_grad, n.active),
        (n.g_both,),
        lambda a, u, b, v: (gradient_product([(a, u), (b, v)], 384),),
        (n.g_sum, n.g_both, to_sum),
    )

    def share(v):
        row = bit("row")
        first, second = halves(v)
        return jnp.where(row, second, first), jnp.where(row, first, second)

    def last_sum(a, b):
        total = a.astype(WIDE) + b.astype(WIDE)
        return total[:, :units], total[:, units:]

    s.g_mlp_row = ((n.g_sum,), (n.g_keep, n.g_give), share, (n.g_got, n.g_give, to_row))
    s.g_mlp_end = ((n.g_keep, n.g_got), (n.grad_up, n.grad_down), last_sum)
    s.act, s.act_go, s.act_on, s.act_on2, s.act_end = line_sums_steps(
        (n.active,),
        (n.full_mlp,),
        (1,),
        lambda a, b, c, x: ((x + plain_total(a, b, c)).astype(LOW),),
        (n.x2,),
        (n.act_local,),
    )
    s.c2_on, s.c2_in, s.d2 = rows_steps(
        n.c2, product_of(3, 1), (n.full_cross,), (n.whole_c2, n.d2)
    )
    s.mix2_back = (
        (n.query2, n.text_kv, n.d2),
        (n.dq2, n.dk2, n.dv2),
        lambda q, kv, d: attention_back((q, 0), (kv, 0), (kv, 1), d, places, False),
    )
    s.h2, s.h2_on, s.h2_end = sums_steps(
        (n.dq2,),
        (n.full_cross,),
        (0,),
        close_norm,
        (n.x1, n.gain1, n.e2),
        (n.e1, n.c1, n.norm1),
        *row_sends(n.c1),
    )
    s.g_cross, s.g_cross_far, s.g_cross_row, s.g_cross_end = gradients_steps(
        (n.whole_cross, n.dq2, n.whole_text, n.dk2, n.whole_text, n.dv2, n.whole_c2, n.mix2),
        [half] * 4,
        (n.grad_cq, n.grad_ck, n.grad_cv, n.grad_cout),
    )
    s.tg, s.tg_on, s.tg_end = sums_steps(
        (n.dk2, n.dv2),
        (n.full_cross, n.full_cross),
        (1, 2),
        lambda *v: (plain_total(*v),),
        (),
        (n.text_sum,),
    )
    s.c1_on, s.c1_in, s.d1 = rows_steps(
        n.c1, product_of(3, 1), (n.full_self,), (n.whole_c1, n.d1)
    )
    s.mix1_back = (
        (n.qkv, n.d1),
        (n.dq1, n.dk1, n.dv1),
        lambda q, d: attention_back((q, 0), (q, 1), (q, 2), d, places, True),
    )
    s.h1, s.h1_on, s.h1_end = sums_steps(
        (n.dq1, n.dk1, n.dv1),
        (n.full_self,) * 3,
        (0, 1, 2),
        close_norm,
        (n.x0, n.gain0, n.e1),
        (n.e0, n.c0, n.norm0),
    )
    s.g_self, s.g_self_far, s.g_self_row, s.g_self_end = gradients_steps(
        (n.whole_self, n.dq1, n.whole_self, n.dk1, n.whole_self, n.dv1, n.whole_c1, n.mix1),
        [half] * 4,
        (n.grad_q, n.grad_k, n.grad_v, n.grad_out),
    )

    def leave(*locals_):
        cut = [halves(regroup(v, 4)) for v in locals_]
        return *[v[0] for v in cut], jnp.concatenate([v[1].astype(LOW) for v in cut], axis=0)

    s.leave = (
        (n.act_local, n.text_sum),
        (n.keep_act, n.keep_text, n.give_o),
        leave,
        (n.got_o, n.give_o, to_far),
    )
    s.sent = ((n.got_o,), (n.got_o2,), keep)
    s.last = ((n.e0,), (n.keep_e, n.give_e), leave, (n.got_e, n.give_e, to_far))

    def narrow(axis, value):
        middle, upper = value.shape[1] // 2, bit(axis)
        low, high = value[:, :middle], value[:, middle:]
        return jnp.where(upper, high, low), jnp.where(upper, low, high)

    def sum_narrow(axis):
        return lambda v, g: narrow(axis, v + g)

    s.s0 = (
        (n.norm0, n.norm1, n.norm2),
        (n.k0, n.w0),
        lambda *v: narrow(axes[4], regroup(jnp.concatenate(v, axis=0), 4)),
        (n.h0, n.w0, moves[4]),
    )
    s.s1 = ((n.k0, n.h0), (n.k1, n.w1), sum_narrow(axes[3]), (n.h1, n.w1, moves[3]))
    s.s2 = ((n.k1, n.h1), (n.k2, n.w2), sum_narrow(axes[2]), (n.h2, n.w2, moves[2]))
    s.s3 = ((n.k2, n.h2), (n.k3, n.w3), sum_narrow(axes[1]), (n.h3, n.w3, moves[1]))
    s.s4 = ((n.k3, n.h3), (n.k4, n.w4), sum_narrow(axes[0]), (n.h4, n.w4, moves[0]))
    s.s5 = ((n.k4, n.h4), (n.norm_sums,), lambda v, g: (v + g,))
    return (
        s.frames,
        s.w_self,
        s.n0,
        s.w_self_far,
        s.w_mlp,
        s.n1,
        s.frames_in,
        s.n2,
        s.n3,
        s.n4,
        s.w_mlp_all,
        s.norm0,
        s.w_self_all,
        s.trade,
        s.w_cross,
        s.a1_on,
        s.w_cross_far,
        s.a1_in,
        s.qkv,
        s.mix1,
        s.w_cross_all,
        s.w_mlp_go,
        s.x1,
        s.x1_on,
        s.both,
        s.text_go,
        s.x1_end,
        s.text_on,
        s.a2_on,
        s.text_in,
        s.text_all,
        s.c3_on,
        s.a2_in,
        s.text_kv,
        s.query2,
        s.mix2,
        s.x2,
        s.x2_on,
        s.c3_on2,
        s.x2_end,
        s.c3_in,
        s.c3_all,
        s.a3_on,
        s.a3_on2,
        s.a3_in,
        s.middle,
        s.h3,
        s.h3_go,
        s.g_mlp,
        s.h3_on,
        s.act,
        s.h3_on2,
        s.h3_end,
        s.c2_on,
        s.c2_in,
        s.act_go,
        s.d2,
        s.mix2_back,
        s.h2,
        s.g_cross,
        s.h2_on,
        s.h2_end,
        s.c1_on,
        s.g_mlp_row,
        s.act_on,
        s.c1_in,
        s.d1,
        s.mix1_back,
        s.g_self,
        s.g_cross_far,
        s.h1,
        s.act_on2,
        s.h1_on,
        s.g_mlp_end,
        s.act_end,
        s.g_cross_row,
        s.g_self_far,
        s.h1_end,
        s.last,
        s.tg,
        s.s0,
        s.s1,
        s.tg_on,
        s.s2,
        s.g_cross_end,
        s.g_self_row,
        s.tg_end,
        s.leave,
        s.s3,
        s.s4,
        s.s5,
        s.sent,
        s.g_self_end,
    )


def on_device_pairs(
    frames,
    text_states,
    self_q,
    self_k,
    self_v,
    self_out,
    cross_q,
    cross_k,
    cross_v,
    cross_out,
    mlp_up,
    mlp_down,
    norm_gains,
    norm_shifts,
    cotangent,
):
    n = Name()
    values = {
        n.frames: frames,
        n.text_states: text_states,
        n.self_q: self_q,
        n.self_k: self_k,
        n.self_v: self_v,
        n.self_out: self_out.T,
        n.cross_q: cross_q,
        n.cross_k: cross_k,
        n.cross_v: cross_v,
        n.cross_out: cross_out.T,
        n.mlp_up: mlp_up,
        n.mlp_down: mlp_down.T,
        n.norm_gains: norm_gains,
        n.norm_shifts: norm_shifts,
        n.cotangent: cotangent,
    }
    order = plan_pairs(
        n, self_q.shape[1], mlp_up.shape[1], frames.shape[1], text_states.shape[1]
    )
    values = run_steps(values, order)
    far_bit, own = bit("far"), frames.shape[1]

    def arrive(own, other):
        other = values[other] if isinstance(other, Name) else other
        own, other = values[own], other.astype(values[own].dtype)
        return jnp.stack([jnp.where(far_bit, other, own), jnp.where(far_bit, own, other)])

    return (
        arrive(n.keep_act, values[n.got_o2][:own]),
        arrive(n.keep_e, n.got_e),
        arrive(n.keep_text, values[n.got_o2][own:]),
        values[n.grad_q],
        values[n.grad_k],
        values[n.grad_v],
        values[n.grad_out].T,
        values[n.grad_cq],
        values[n.grad_ck],
        values[n.grad_cv],
        values[n.grad_cout].T,
        values[n.grad_up],
        values[n.grad_down].T,
        values[n.norm_sums][::2],
        values[n.norm_sums][1::2],
    )


def solution(mesh):
    paired = dict(mesh.shape) == {"dp": 8, "tensor": 4}
    names = ("row", "column", "core", "far", "near")
    dp, tensor = (names[:3], names[3:]) if paired else (("dp",), ("tensor",))
    rows = P(dp, tensor, None)
    into = P(dp, tensor)
    out_of = P(tensor, dp)
    norms = P(None, dp + tensor)
    weights = (into, into, into, out_of, into, into, into, out_of, into, out_of)
    return jax.shard_map(
        on_device_pairs if paired else on_device,
        mesh=Mesh(mesh.devices.reshape((2,) * 5), names) if paired else mesh,
        in_specs=(rows, rows, *weights, norms, norms, rows),
        out_specs=(rows, rows, rows, *weights, norms, norms),
        check_vma=False,
    )
```

```python
import functools
import math

import jax
import jax.numpy as jnp
from jax import lax
from jax.experimental import pallas as pl
from jax.experimental.pallas import tpu as pltpu
from jax.sharding import Mesh, PartitionSpec as P

HEAD_DIM = 64
EPS = 1e-05
LOW = jnp.bfloat16
WIDE = jnp.float32


def norm_forward(values, gain, shift):
    average = jnp.mean(values, axis=-1, keepdims=True)
    centered = values - average
    variance = jnp.mean(centered * centered, axis=-1, keepdims=True)
    inverse = lax.rsqrt(variance + EPS)
    unit = centered * inverse
    return unit * gain + shift, unit, inverse


def norm_back(unit, inverse, gain, upstream):
    scaled = upstream * gain
    mean_scaled = jnp.mean(scaled, axis=-1, keepdims=True)
    mean_product = jnp.mean(scaled * unit, axis=-1, keepdims=True)
    change = inverse * (scaled - mean_scaled - unit * mean_product)
    return change, jnp.sum(upstream * unit, axis=0), jnp.sum(upstream, axis=0)


def gelu_exact(values):
    return jax.nn.gelu(values, approximate=False)


def product(operand, matrix):
    return jnp.dot(operand, matrix, preferred_element_type=WIDE)


def product_left(operand, matrix):
    return lax.dot_general(operand, matrix, (((0,), (0,)), ((), ())), preferred_element_type=WIDE)


def product_right(operand, matrix):
    return lax.dot_general(operand, matrix, (((1,), (1,)), ((), ())), preferred_element_type=WIDE)


def swap(value, axis, stride):
    size = lax.axis_size(axis)
    return lax.ppermute(value, axis, [(i, i ^ stride) for i in range(size)])


def levels():
    found, stride = [], 1
    for axis in ("tensor", "dp"):
        step = 1
        while step < lax.axis_size(axis):
            found.append((axis, step))
            step *= 2
    return found


def gather_small(value):
    for axis, step in levels():
        upper = (lax.axis_index(axis) // step) % 2 == 1
        other = swap(value, axis, step)
        value = jnp.where(
            upper,
            jnp.concatenate([other, value], axis=-1),
            jnp.concatenate([value, other], axis=-1),
        )
    return value


def scatter_small(value):
    for axis, step in reversed(levels()):
        upper = (lax.axis_index(axis) // step) % 2 == 1
        half = value.shape[-1] // 2
        low, high = value[..., :half], value[..., half:]
        other = swap(jnp.where(upper, low, high), axis, step)
        value = jnp.where(upper, high, low) + other
    return value


def spread(local):
    gathered = lax.all_gather(local, "tensor", axis=0, tiled=False)
    return gathered.reshape(-1, local.shape[-1])


def collect(partial, shape):
    summed = lax.psum_scatter(
        partial.astype(LOW), "tensor", scatter_dimension=0, tiled=True
    )
    return summed.astype(WIDE)


def by_heads(rows, count, seqs):
    frames = rows.shape[0] // (count * seqs)
    split = rows.reshape(count, seqs, frames, -1, HEAD_DIM)
    return split.transpose(1, 3, 0, 2, 4).reshape(seqs, -1, count * frames, HEAD_DIM)


def by_rows(heads, count, seqs):
    frames = heads.shape[2] // count
    split = heads.reshape(seqs, heads.shape[1], count, frames, HEAD_DIM)
    return split.transpose(2, 0, 3, 1, 4).reshape(count * seqs * frames, -1)


def weights_of(queries, keys, causal):
    scores = jnp.einsum("shqd,shkd->shqk", queries, keys, preferred_element_type=WIDE)
    scores = scores * HEAD_DIM**-0.5
    if causal:
        length = queries.shape[2]
        visible = jnp.arange(length)[:, None] >= jnp.arange(length)[None, :]
        scores = jnp.where(visible, scores, -1e30)
    largest = jnp.max(scores, axis=-1, keepdims=True)
    raw = jnp.exp(scores - largest)
    return raw / jnp.sum(raw, axis=-1, keepdims=True)


def attend(queries, keys, values, causal):
    chance = weights_of(queries, keys, causal).astype(LOW)
    return jnp.einsum("shqk,shkd->shqd", chance, values, preferred_element_type=WIDE).astype(LOW)


def attend_back(queries, keys, values, upstream, causal):
    chance = weights_of(queries, keys, causal)
    grad = jnp.einsum("shqd,shkd->shqk", upstream, values, preferred_element_type=WIDE)
    dots = jnp.sum(chance * grad, axis=-1, keepdims=True)
    score_grad = (chance * (grad - dots)).astype(LOW)
    scaling = HEAD_DIM**-0.5
    grad_q = jnp.einsum("shqk,shkd->shqd", score_grad, keys, preferred_element_type=WIDE)
    grad_k = jnp.einsum("shqk,shqd->shkd", score_grad, queries, preferred_element_type=WIDE)
    grad_v = jnp.einsum("shqk,shqd->shkd", chance.astype(LOW), upstream, preferred_element_type=WIDE)
    return (grad_q * scaling).astype(LOW), (grad_k * scaling).astype(LOW), grad_v.astype(LOW)


def on_device(
    frames,
    text_states,
    self_q,
    self_k,
    self_v,
    self_out,
    cross_q,
    cross_k,
    cross_v,
    cross_out,
    mlp_up,
    mlp_down,
    norm_gains,
    norm_shifts,
    cotangent,
):
    seqs, own, width = frames.shape
    text_own = text_states.shape[1]
    count = lax.axis_size("tensor")
    inner = self_q.shape[1]

    norms = gather_small(jnp.concatenate([norm_gains, norm_shifts], axis=0))
    gains, shifts = norms[:3], norms[3:]

    whole_grad = spread(cotangent.reshape(-1, width))
    whole_text = spread(text_states.reshape(-1, width))

    def gather(parts):
        joined = parts[0] if len(parts) == 1 else jnp.concatenate(parts, axis=1)
        return lax.all_gather(joined, "dp", axis=0, tiled=True)

    full_qkv = gather([self_q, self_k, self_v])
    full_mid = gather([self_out.T, cross_q, cross_k, cross_v, cross_out.T])
    full_mlp = gather([mlp_up, mlp_down.T])
    full_out = full_mid[:, :inner]
    full_cq = full_mid[:, inner : 2 * inner]
    full_ckv = full_mid[:, 2 * inner : 4 * inner]
    full_cout = full_mid[:, 4 * inner :]
    hidden_own = mlp_up.shape[1]
    full_up, full_down = full_mlp[:, :hidden_own], full_mlp[:, hidden_own:]

    x0 = frames.reshape(-1, width).astype(WIDE)
    a1, unit0, inverse0 = norm_forward(x0, gains[0], shifts[0])
    whole_self = spread(a1.astype(LOW))
    qkv = product(whole_self, full_qkv).astype(LOW)
    query1 = by_heads(qkv[:, :inner], count, seqs)
    key1 = by_heads(qkv[:, inner : 2 * inner], count, seqs)
    value1 = by_heads(qkv[:, 2 * inner :], count, seqs)
    mix1 = by_rows(attend(query1, key1, value1, True), count, seqs)
    x1 = x0 + collect(product_right(mix1, full_out), None)

    a2, unit1, inverse1 = norm_forward(x1, gains[1], shifts[1])
    whole_cross = spread(a2.astype(LOW))
    query2 = by_heads(product(whole_cross, full_cq).astype(LOW), count, seqs)
    text_kv = product(whole_text, full_ckv).astype(LOW)
    key2 = by_heads(text_kv[:, :inner], count, seqs)
    value2 = by_heads(text_kv[:, inner:], count, seqs)
    mix2 = by_rows(attend(query2, key2, value2, False), count, seqs)
    x2 = x1 + collect(product_right(mix2, full_cout), None)

    a3, unit2, inverse2 = norm_forward(x2, gains[2], shifts[2])
    whole_mlp = spread(a3.astype(LOW))
    hidden = product(whole_mlp, full_up)
    active_grad = product(whole_grad, full_down)
    active, pullback = jax.vjp(gelu_exact, hidden)
    active = active.astype(LOW)
    hidden_low = pullback(active_grad)[0].astype(LOW)
    h3 = collect(product_right(hidden_low, full_up), None)
    activations = (x2 + collect(product_right(active, full_down), None)).astype(LOW)

    def reduce(parts):
        joined = parts[0] if len(parts) == 1 else jnp.concatenate(parts, axis=1)
        return lax.psum_scatter(joined, "dp", scatter_dimension=0, tiled=True).astype(WIDE)

    sum_mlp = reduce(
        [
            product_left(whole_mlp, hidden_low).astype(LOW),
            product_left(whole_grad, active).astype(LOW),
        ]
    )

    e3 = cotangent.reshape(-1, width).astype(WIDE)
    change, gain2, shift2 = norm_back(unit2, inverse2, gains[2], h3)
    e2 = e3 + change
    whole_c2 = spread(e2.astype(LOW))
    d2 = by_heads(product(whole_c2, full_cout).astype(LOW), count, seqs)
    grad_q2, grad_k2, grad_v2 = attend_back(query2, key2, value2, d2, False)
    grad_q2 = by_rows(grad_q2, count, seqs)
    grad_kv2 = jnp.concatenate(
        [by_rows(grad_k2, count, seqs), by_rows(grad_v2, count, seqs)], axis=1
    )
    h2 = collect(product_right(grad_q2, full_cq), None)
    grad_text = collect(product_right(grad_kv2, full_ckv), None)
    sum_cross = reduce(
        [
            product_left(whole_cross, grad_q2).astype(LOW),
            product_left(whole_text, grad_kv2).astype(LOW),
            product_left(whole_c2, mix2).astype(LOW),
        ]
    )

    change, gain1, shift1 = norm_back(unit1, inverse1, gains[1], h2)
    e1 = e2 + change
    whole_c1 = spread(e1.astype(LOW))
    d1 = by_heads(product(whole_c1, full_out).astype(LOW), count, seqs)
    grads = attend_back(query1, key1, value1, d1, True)
    grad_qkv = jnp.concatenate([by_rows(part, count, seqs) for part in grads], axis=1)
    h1 = collect(product_right(grad_qkv, full_qkv), None)
    sum_self = reduce(
        [
            product_left(whole_self, grad_qkv).astype(LOW),
            product_left(whole_c1, mix1).astype(LOW),
        ]
    )
    change, gain0, shift0 = norm_back(unit0, inverse0, gains[0], h1)
    grad_frames = e1 + change

    norm_sums = scatter_small(jnp.stack([gain0, gain1, gain2, shift0, shift1, shift2]))

    def cut(joined, index):
        return joined[:, index * inner : (index + 1) * inner]

    return (
        activations.reshape(frames.shape),
        grad_frames.reshape(frames.shape),
        grad_text.reshape(text_states.shape),
        cut(sum_self, 0),
        cut(sum_self, 1),
        cut(sum_self, 2),
        cut(sum_self, 3).T,
        cut(sum_cross, 0),
        cut(sum_cross, 1),
        cut(sum_cross, 2),
        cut(sum_cross, 3).T,
        sum_mlp[:, :hidden_own],
        sum_mlp[:, hidden_own:].T,
        norm_sums[:3],
        norm_sums[3:],
    )


def exchange(value, axis):
    return lax.ppermute(value, axis, [(0, 1), (1, 0)])


def bit(axis):
    return lax.axis_index(axis) == 1


def ordered(flag, own, other, axis):
    return jnp.where(
        flag,
        jnp.concatenate([other, own], axis=axis),
        jnp.concatenate([own, other], axis=axis),
    )


def regroup(value, outer):
    width, inner = value.shape[-1] // 8, 8 // outer
    parts = [value[..., i * width : (i + 1) * width] for i in range(8)]
    order = [parts[o * inner + i] for i in range(inner) for o in range(outer)]
    return jnp.concatenate(order, axis=-1)


def halves(v):
    half = v.shape[0] // 2
    return v[:half], v[half:]


def join(parts, axis):
    return parts[0] if len(parts) == 1 else jnp.concatenate(parts, axis=axis)


VMEM_BYTES = 40 << 20


def whole_block(shape):
    return pl.BlockSpec(shape, lambda *i: (0,) * len(shape), pipeline_mode=pl.Buffered(1))


def settings():
    return dict(
        cost_estimate=pl.CostEstimate(flops=1, bytes_accessed=1, transcendentals=0),
        compiler_params=pltpu.CompilerParams(vmem_limit_bytes=VMEM_BYTES),
    )


def fill(pieces, whole_ref):
    start = 0
    for piece in pieces:
        whole_ref[start : start + piece.shape[0], :] = piece[...]
        start += piece.shape[0]


def rows_product(pieces, weights, first, count, tile):
    depth = weights.shape[0]
    rows = sum(p.shape[0] for p in pieces)

    def body(*refs):
        w_ref, whole_ref, out_ref = refs[len(pieces) :]

        @pl.when(pl.program_id(0) == 0)
        def _():
            fill(refs[: len(pieces)], whole_ref)

        out_ref[...] = jnp.dot(
            whole_ref[...], w_ref[...], preferred_element_type=WIDE
        ).astype(LOW)

    return pl.pallas_call(
        body,
        grid=(count // tile,),
        in_specs=[whole_block(p.shape) for p in pieces]
        + [pl.BlockSpec((depth, tile), lambda j: (0, first + j))],
        out_specs=[
            pl.BlockSpec((rows, depth), lambda j: (0, 0)),
            pl.BlockSpec((rows, tile), lambda j: (0, j)),
        ],
        out_shape=[
            jax.ShapeDtypeStruct((rows, depth), LOW),
            jax.ShapeDtypeStruct((rows, count), LOW),
        ],
        name="rows_product",
        **settings(),
    )(*pieces, weights)


def middle_kernel(*refs):
    pieces, (up_ref, down_ref, grad_ref, whole_ref, active_ref, low_ref) = refs[:7], refs[7:]

    @pl.when(pl.program_id(0) == 0)
    def _():
        fill(line_pieces([piece[...] for piece in pieces]), whole_ref)

    hidden = jnp.dot(whole_ref[...], up_ref[...], preferred_element_type=WIDE)
    upstream = jnp.dot(grad_ref[...], down_ref[...], preferred_element_type=WIDE)
    share = 0.5 + 0.5 * lax.erf(hidden * 0.5**0.5)
    density = jnp.exp(-0.5 * hidden * hidden) * (2.0 * math.pi) ** -0.5
    active_ref[...] = (hidden * share).astype(LOW)
    low_ref[...] = (upstream * (share + hidden * density)).astype(LOW)


def middle(pieces, weights, grad, tile):
    depth, count = weights.shape[0], weights.shape[1] // 2
    rows = grad.shape[0]
    tiles = count // tile
    out = pl.BlockSpec((rows, tile), lambda j: (0, j))
    return pl.pallas_call(
        middle_kernel,
        grid=(tiles,),
        in_specs=[whole_block(p.shape) for p in pieces]
        + [
            pl.BlockSpec((depth, tile), lambda j: (0, j)),
            pl.BlockSpec((depth, tile), lambda j: (0, tiles + j)),
            whole_block(grad.shape),
        ],
        out_specs=[pl.BlockSpec((rows, depth), lambda j: (0, 0)), out, out],
        out_shape=[jax.ShapeDtypeStruct((rows, n), LOW) for n in (depth, count, count)],
        name="middle",
        **settings(),
    )(*pieces, weights, weights, grad)


def pieces_product(terms, tile, cuts=(2, 2, 2, 1, 1)):
    rows, depth = terms[0][0].shape[0], terms[0][1].shape[0]
    unit = rows // sum(cuts)

    def body(*refs):
        total = None
        for i in range(len(terms)):
            term = lax.dot_general(
                refs[2 * i][...],
                refs[2 * i + 1][...],
                (((1,), (1,)), ((), ())),
                preferred_element_type=WIDE,
            )
            total = term if total is None else total + term
        fill_from = 0
        for ref in refs[2 * len(terms) :]:
            ref[...] = total[fill_from : fill_from + ref.shape[0]].astype(LOW)
            fill_from += ref.shape[0]

    specs, operands = [], []
    for x, w, block in terms:
        specs.append(whole_block(x.shape))
        specs.append(pl.BlockSpec((tile, x.shape[1]), lambda i, block=block: (i, block)))
        operands += [x, w]
    sizes = [unit * cut for cut in cuts]
    return pl.pallas_call(
        body,
        grid=(depth // tile,),
        in_specs=specs,
        out_specs=[pl.BlockSpec((n, tile), lambda i: (0, i)) for n in sizes],
        out_shape=[jax.ShapeDtypeStruct((n, depth), LOW) for n in sizes],
        name="pieces_product",
        **settings(),
    )(*operands)


def gradient_product(pairs, tile):
    depth = pairs[0][0].shape[1]
    tiles = [u.shape[1] // tile for _, u in pairs]
    starts = [sum(tiles[:i]) for i in range(len(tiles))]

    def body(*refs):
        out_ref, j = refs[-1], pl.program_id(0)
        for i in range(len(pairs)):

            @pl.when((j >= starts[i]) & (j < starts[i] + tiles[i]))
            def _(i=i):
                out_ref[...] = product_left(refs[2 * i][...], refs[2 * i + 1][...]).astype(LOW)

    specs, operands = [], []
    for (a, u), start, count in zip(pairs, starts, tiles):
        specs.append(whole_block(a.shape))
        specs.append(
            pl.BlockSpec(
                (u.shape[0], tile),
                lambda j, start=start, count=count: (0, jnp.clip(j - start, 0, count - 1)),
            )
        )
        operands += [a, u]
    return pl.pallas_call(
        body,
        grid=(sum(tiles),),
        in_specs=specs,
        out_specs=pl.BlockSpec((depth, tile), lambda j: (0, j)),
        out_shape=jax.ShapeDtypeStruct((depth, tile * sum(tiles)), LOW),
        name="gradient_product",
        **settings(),
    )(*operands)


def relay_kernel(near_ref, row_ref, one_ref, two_ref, near_out, row_out):
    half = one_ref.shape[0]
    near_out[:half] = (near_ref[:half].astype(WIDE) + one_ref[...].astype(WIDE)).astype(LOW)
    near_out[half:] = near_ref[half:]
    row_out[:half] = row_ref[:half]
    row_out[half:] = (row_ref[half:].astype(WIDE) + two_ref[...].astype(WIDE)).astype(LOW)


def relay_sums(near, row, one, two):
    return pl.pallas_call(
        relay_kernel,
        out_shape=[jax.ShapeDtypeStruct(near.shape, LOW)] * 2,
        name="relay_sums",
        **settings(),
    )(near, row, one, two)


def open_kernel(own_ref, near_ref, row_ref, x_ref, gain_ref, shift_ref, x_out, a_out):
    total = own_ref[...].astype(WIDE) + near_ref[...].astype(WIDE) + row_ref[...].astype(WIDE)
    x = x_ref[...] + total
    x_out[...] = x
    a_out[...] = norm_forward(x, gain_ref[...], shift_ref[...])[0].astype(LOW)


def open_norm(own, near, row, x, gain, shift):
    return pl.pallas_call(
        open_kernel,
        out_shape=[jax.ShapeDtypeStruct(x.shape, WIDE), jax.ShapeDtypeStruct(x.shape, LOW)],
        name="open_norm",
        **settings(),
    )(own, near, row, x, gain, shift)


def close_kernel(own_ref, near_ref, row_ref, x_ref, gain_ref, e_ref, e_out, c_out, sums_out):
    total = own_ref[...].astype(WIDE) + near_ref[...].astype(WIDE) + row_ref[...].astype(WIDE)
    _, unit, inverse = norm_forward(x_ref[...], gain_ref[...], 0.0)
    change, gain_grad, shift_grad = norm_back(unit, inverse, gain_ref[...], total)
    e = e_ref[...].astype(WIDE) + change
    e_out[...] = e
    c_out[...] = e.astype(LOW)
    sums_out[...] = jnp.concatenate([gain_grad[None], shift_grad[None]], axis=0)


def close_norm(own, near, row, x, gain, e):
    return pl.pallas_call(
        close_kernel,
        out_shape=[
            jax.ShapeDtypeStruct(x.shape, WIDE),
            jax.ShapeDtypeStruct(x.shape, LOW),
            jax.ShapeDtypeStruct((2, x.shape[1]), WIDE),
        ],
        name="close_norm",
        **settings(),
    )(own, near, row, x, gain, e)


def plain_total(a, b, c):
    return a.astype(WIDE) + b.astype(WIDE) + c.astype(WIDE)


def head_weights(queries, keys, mask):
    scores = lax.dot_general(queries, keys, (((1,), (1,)), ((), ())), preferred_element_type=WIDE)
    scores = scores * HEAD_DIM**-0.5
    if mask is not None:
        scores = jnp.where(mask, scores, -1e30)
    raw = jnp.exp(scores - jnp.max(scores, axis=-1, keepdims=True))
    return raw * (1.0 / jnp.sum(raw, axis=-1, keepdims=True))


def attend_kernel(heads, causal, q_ref, k_ref, v_ref, down_ref, along_ref, out_ref):
    mask = down_ref[...] >= along_ref[...] if causal else None
    for head in range(heads):
        columns = slice(head * HEAD_DIM, (head + 1) * HEAD_DIM)
        chance = head_weights(q_ref[:, columns], k_ref[:, columns], mask)
        mixed = jnp.dot(chance.astype(LOW), v_ref[:, columns], preferred_element_type=WIDE)
        out_ref[:, columns] = mixed.astype(LOW)


def attend_back_kernel(
    heads, causal, q_ref, k_ref, v_ref, up_ref, down_ref, along_ref, dq_ref, dk_ref, dv_ref
):
    mask = down_ref[...] >= along_ref[...] if causal else None
    scaling = HEAD_DIM**-0.5
    for head in range(heads):
        columns = slice(head * HEAD_DIM, (head + 1) * HEAD_DIM)
        queries, keys, upstream = q_ref[:, columns], k_ref[:, columns], up_ref[:, columns]
        chance = head_weights(queries, keys, mask)
        grad = lax.dot_general(
            upstream, v_ref[:, columns], (((1,), (1,)), ((), ())), preferred_element_type=WIDE
        )
        dots = jnp.sum(chance * grad, axis=-1, keepdims=True)
        score_grad = (chance * (grad - dots)).astype(LOW)
        dq_ref[:, columns] = (
            jnp.dot(score_grad, keys, preferred_element_type=WIDE) * scaling
        ).astype(LOW)
        dk_ref[:, columns] = (product_left(score_grad, queries) * scaling).astype(LOW)
        dv_ref[:, columns] = product_left(chance.astype(LOW), upstream).astype(LOW)


def column_block(rows, width, index):
    return pl.BlockSpec((rows, width), lambda s: (s, index))


def attention(queries, keys, values, places, causal):
    width = places[2]
    rows, key_rows = queries[0].shape[0] // 2, keys[0].shape[0] // 2
    heads = width // HEAD_DIM
    return pl.pallas_call(
        functools.partial(attend_kernel, heads, causal),
        grid=(2,),
        in_specs=[
            column_block(rows, width, queries[1]),
            column_block(key_rows, width, keys[1]),
            column_block(key_rows, width, values[1]),
            pl.BlockSpec(places[0].shape, lambda s: (0, 0)),
            pl.BlockSpec(places[1].shape, lambda s: (0, 0)),
        ],
        out_specs=column_block(rows, width, 0),
        out_shape=jax.ShapeDtypeStruct((2 * rows, width), LOW),
        **settings(),
        name="attend",
    )(queries[0], keys[0], values[0], places[0], places[1])


def attention_back(queries, keys, values, upstream, places, causal):
    width = places[2]
    rows, key_rows = queries[0].shape[0] // 2, keys[0].shape[0] // 2
    heads = width // HEAD_DIM
    return pl.pallas_call(
        functools.partial(attend_back_kernel, heads, causal),
        grid=(2,),
        in_specs=[
            column_block(rows, width, queries[1]),
            column_block(key_rows, width, keys[1]),
            column_block(key_rows, width, values[1]),
            column_block(rows, width, 0),
            pl.BlockSpec(places[0].shape, lambda s: (0, 0)),
            pl.BlockSpec(places[1].shape, lambda s: (0, 0)),
        ],
        out_specs=[
            column_block(rows, width, 0),
            column_block(key_rows, width, 0),
            column_block(key_rows, width, 0),
        ],
        out_shape=[
            jax.ShapeDtypeStruct((2 * rows, width), LOW),
            jax.ShapeDtypeStruct((2 * key_rows, width), LOW),
            jax.ShapeDtypeStruct((2 * key_rows, width), LOW),
        ],
        **settings(),
        name="attend_back",
    )(queries[0], keys[0], values[0], upstream, places[0], places[1])


def line_pieces(pieces):
    local, d1, u3, d2, u2, u1, d3 = pieces
    return local, d1 + u3, d2 + u2, u1 + d3


class Name:
    def __getattr__(self, key):
        return self.__dict__.setdefault(key, Name())


def swapping(axis):
    return lambda v: exchange(v, axis)


def stepping(*perm):
    return lambda v: lax.ppermute(v, ("far", "near"), perm)


to_row, to_column, to_core = swapping("row"), swapping("column"), swapping("core")
to_far, to_near = swapping("far"), swapping("near")
up_all, up_last2, up_last = stepping((0, 1), (1, 2), (2, 3)), stepping((1, 2), (2, 3)), stepping((2, 3))
up_first, up_first2 = stepping((0, 1)), stepping((0, 1), (1, 2))
down_all, down_last2, down_last = (
    stepping((3, 2), (2, 1), (1, 0)),
    stepping((2, 1), (1, 0)),
    stepping((1, 0)),
)
down_first, down_first2 = stepping((3, 2)), stepping((3, 2), (2, 1))


def to_all(v):
    return lax.all_gather(v, ("column", "core"), axis=0, tiled=True)


def to_sum(v):
    return lax.psum_scatter(v, ("column", "core"), scatter_dimension=0, tiled=True)


def run_steps(values, order):
    last = None
    for needs, gives, work, *sends in order:
        taken = [values[n] for n in needs]
        if last is not None:
            taken, _ = lax.optimization_barrier((taken, last))
        last = work(*taken)
        values.update(zip(gives, last, strict=True))
        for result, source, move in sends:
            values[result] = move(values[source])
    return values


def keep(*values):
    return values


def row_sends(local):
    return (local.row, local, to_row), (local.near, local, to_near)


def rows_steps(local, work, needs, gives):
    def relay(row, near):
        return halves(row)[0], halves(near)[1]

    return (
        (
            (local.row, local.near),
            (local.p, local.q),
            relay,
            (local.one, local.p, to_near),
            (local.two, local.q, to_row),
        ),
        ((local.one, local.two), (local.three, local.four), keep),
        (
            (local, local.near, local.row, local.three, local.four, *needs),
            gives,
            lambda *v: work(v[:5], *v[5:]),
        ),
    )


def line_sends(local):
    return (local.u1, local, up_all), (local.d1, local, down_all)


def line_rows_steps(local, work, needs, gives):
    c = local
    return (
        ((c.u1, c.d1), (c.v1, c.w1), keep, (c.u2, c.v1, up_last2), (c.d2, c.w1, down_last2)),
        ((c.u2, c.d2), (c.v2, c.w2), keep, (c.u3, c.v2, up_last), (c.d3, c.w2, down_last)),
        ((c.u3, c.d3), (c.v3, c.w3), keep),
        (
            (c, c.w1, c.v3, c.w2, c.v2, c.v1, c.w3, *needs),
            gives,
            lambda *u: work(u[:7], *u[7:]),
        ),
    )


def line_sums_steps(terms, weights, blocks, work, needs, gives, *sends):
    count, c = len(terms), Name()

    def start(*v):
        return pieces_product(list(zip(v[:count], v[count:], blocks)), 384, (1, 1, 1, 1))

    def add(a, b, c, d):
        return (
            (a.astype(WIDE) + b.astype(WIDE)).astype(LOW),
            (c.astype(WIDE) + d.astype(WIDE)).astype(LOW),
        )

    return (
        ((*terms, *weights), (c.q0, c.q1, c.q2, c.q3), start),
        (
            (c.q0, c.q1, c.q2, c.q3),
            (c.p0, c.p1, c.p2, c.p3),
            keep,
            (c.d3, c.p1, down_first),
            (c.u3, c.p3, up_first),
        ),
        (
            (c.p2, c.d3, c.p2, c.u3),
            (c.a2, c.b2),
            add,
            (c.d2, c.a2, down_first2),
            (c.u2, c.b2, up_first2),
        ),
        (
            (c.p3, c.d2, c.p1, c.u2),
            (c.a1, c.b1),
            add,
            (c.d1, c.a1, down_all),
            (c.u1, c.b1, up_all),
        ),
        ((c.p0, c.d1, c.u1, *needs), gives, work, *sends),
    )


def sums_steps(terms, weights, blocks, work, needs, gives, *sends):
    count, c = len(terms), Name()

    def start(*v):
        return pieces_product(list(zip(v[:count], v[count:], blocks)), 384)

    return (
        (
            (*terms, *weights),
            (c.own, c.n, c.r, c.one, c.two),
            start,
            (c.a, c.one, to_row),
            (c.b, c.two, to_near),
        ),
        (
            (c.n, c.r, c.a, c.b),
            (c.c, c.d),
            relay_sums,
            (c.x, c.c, to_near),
            (c.y, c.d, to_row),
        ),
        ((c.own, c.x, c.y, *needs), gives, work, *sends),
    )


def weights_steps(parts, cuts, full):
    c = Name()

    def split(*shards):
        row = bit("row")
        lows = join([p[:, :w] for p, w in zip(shards, cuts)], 1)
        highs = join([p[:, w:] for p, w in zip(shards, cuts)], 1)
        return jnp.where(row, highs, lows), jnp.where(row, lows, highs)

    def stack(own, got):
        return (ordered(bit("row"), own, got, 0),)

    def side_by_side(own, other):
        pieces, start = [], 0
        for w in cuts:
            pieces += [own[:, start : start + w], other[:, start : start + w]]
            start += w
        return (jnp.concatenate(pieces, axis=1),)

    return (
        (parts, (c.a, c.b), split, (c.c, c.b, to_row)),
        ((c.a, c.c), (c.d,), stack, (c.e, c.d, to_far)),
        ((c.d, c.e), (c.f,), side_by_side, (full, c.f, to_all)),
    )


def gradients_steps(pairs, cuts, gives):
    n = Name()

    def make(*v):
        return (gradient_product(list(zip(v[::2], v[1::2])), 384),)

    def cut_far(total):
        stay, leave, start = [], [], 0
        for c in cuts:
            stay.append(total[:, start : start + c])
            leave.append(total[:, start + c : start + 2 * c])
            start += 2 * c
        return join(stay, 1), join(leave, 1)

    def cut_row(own, got):
        total, row = own.astype(WIDE) + got.astype(WIDE), bit("row")
        first, second = halves(total)
        return jnp.where(row, second, first), jnp.where(row, first, second).astype(LOW)

    def place(own, got):
        got, row = got.astype(WIDE), bit("row")
        found, start = [], 0
        for c in cuts:
            found.append(ordered(row, own[:, start : start + c], got[:, start : start + c], 1))
            start += c
        return found

    return (
        (pairs, (n.a,), make, (n.b, n.a, to_sum)),
        ((n.b,), (n.c, n.d), cut_far, (n.e, n.d, to_far)),
        ((n.c, n.e), (n.f, n.g), cut_row, (n.h, n.g, to_row)),
        ((n.f, n.h), gives, place),
    )


def plan_pairs(n, inner, units, own_frames, own_text):
    s, far_bit = Name(), bit("far")

    def divide(v):
        return jnp.where(far_bit, v[1], v[0]), jnp.where(far_bit, v[0], v[1])

    half, wide = inner // 2, units // 2
    s.frames = ((n.frames,), (n.keep_f, n.give_f), divide, (n.got_f, n.give_f, to_far))
    s.frames_in = ((n.got_f,), (n.got_f2,), keep)
    s.w_self, s.w_self_far, s.w_self_all = weights_steps(
        (n.self_q, n.self_k, n.self_v, n.self_out), [half] * 4, n.full_self
    )
    s.w_cross, s.w_cross_far, s.w_cross_all = weights_steps(
        (n.cross_q, n.cross_k, n.cross_v, n.cross_out), [half] * 4, n.full_cross
    )
    s.w_mlp = (
        (n.mlp_up, n.mlp_down),
        (n.own_mlp,),
        lambda a, b: (jnp.concatenate([a, b], axis=1),),
        (n.got_mlp, n.own_mlp, to_row),
    )
    s.w_mlp_all = (
        (n.own_mlp, n.got_mlp),
        (n.both_mlp,),
        lambda a, b: (ordered(bit("row"), a, b, 0),),
    )
    s.w_mlp_go = ((n.both_mlp,), (n.both_mlp2,), keep, (n.full_mlp, n.both_mlp2, to_all))

    axes, moves = ("near", "far", "core", "column", "row"), (to_near, to_far, to_core, to_column, to_row)

    def widen(axis):
        return lambda o, g: (ordered(bit(axis), o, g, 1),)

    s.n0 = (
        (n.norm_gains, n.norm_shifts),
        (n.v0,),
        lambda a, b: (jnp.concatenate([a, b], axis=0),),
        (n.g0, n.v0, moves[0]),
    )
    s.n1 = ((n.v0, n.g0), (n.v1,), widen(axes[0]), (n.g1, n.v1, moves[1]))
    s.n2 = ((n.v1, n.g1), (n.v2,), widen(axes[1]), (n.g2, n.v2, moves[2]))
    s.n3 = ((n.v2, n.g2), (n.v3,), widen(axes[2]), (n.g3, n.v3, moves[3]))
    s.n4 = ((n.v3, n.g3), (n.v4,), widen(axes[3]), (n.g4, n.v4, moves[4]))

    def open_rows(kept, got, v, g):
        norms = regroup(ordered(bit("row"), v, g, 1), 2)
        x0 = regroup(jnp.concatenate([kept, got], axis=0), 2).astype(WIDE)
        found = [norms[i : i + 1] for i in range(6)]
        return x0, norm_forward(x0, found[0], found[3])[0].astype(LOW), *found

    s.norm0 = (
        (n.keep_f, n.got_f2, n.v4, n.g4),
        (n.x0, n.a1, n.gain0, n.gain1, n.gain2, n.shift0, n.shift1, n.shift2),
        open_rows,
        *row_sends(n.a1),
    )

    near, far = lax.axis_index("near"), lax.axis_index("far")
    starts = [2 * far + near, 2 * (1 - far) + near, 2 * far + 1 - near, 2 * (1 - far) + 1 - near]
    steps = jnp.arange(own_frames, dtype=jnp.int32)
    position = jnp.concatenate([start * own_frames + steps for start in starts])
    places = (position[:, None], position[None, :], inner)

    def part_ways(t, c):
        return [jnp.concatenate(v, axis=0) for v in zip(divide(t), divide(c))]

    def trade(kept, got):
        text = jnp.concatenate([kept[:own_text], got[:own_text]], axis=0)
        grad = jnp.concatenate([kept[own_text:], got[own_text:]], axis=0)
        return regroup(text, 2), regroup(grad, 2)

    def gathered(pieces):
        return (jnp.concatenate(pieces, axis=0),)

    s.trade = (
        (n.text_states, n.cotangent),
        (n.keep_b, n.give_b),
        part_ways,
        (n.got_b, n.give_b, to_far),
    )
    s.both = ((n.keep_b, n.got_b), (n.text0, n.c3), trade, *line_sends(n.c3))
    s.text_go = ((n.text0,), (n.text,), keep, *row_sends(n.text))
    s.text_on, s.text_in, s.text_all = rows_steps(n.text, gathered, (), (n.whole_text,))
    s.c3_on, s.c3_on2, s.c3_in, s.c3_all = line_rows_steps(
        n.c3, lambda p: gathered(line_pieces(p)), (), (n.whole_grad,)
    )

    def product_of(first, count):
        return lambda p, w: rows_product(p, w, first, count * inner, inner)

    s.a1_on, s.a1_in, s.qkv = rows_steps(
        n.a1, product_of(0, 3), (n.full_self,), (n.whole_self, n.qkv)
    )
    s.mix1 = (
        (n.qkv,),
        (n.mix1,),
        lambda q: (attention((q, 0), (q, 1), (q, 2), places, True),),
    )
    s.x1, s.x1_on, s.x1_end = sums_steps(
        (n.mix1,),
        (n.full_self,),
        (3,),
        open_norm,
        (n.x0, n.gain1, n.shift1),
        (n.x1, n.a2),
        *row_sends(n.a2),
    )
    s.a2_on, s.a2_in, s.query2 = rows_steps(
        n.a2, product_of(0, 1), (n.full_cross,), (n.whole_cross, n.query2)
    )
    s.text_kv = (
        (n.whole_text, n.full_cross),
        (n.text_kv,),
        lambda a, w: rows_product([a], w, 1, 2 * inner, inner)[1:],
    )
    s.mix2 = (
        (n.query2, n.text_kv),
        (n.mix2,),
        lambda q, kv: (attention((q, 0), (kv, 0), (kv, 1), places, False),),
    )
    s.x2, s.x2_on, s.x2_end = sums_steps(
        (n.mix2,),
        (n.full_cross,),
        (3,),
        open_norm,
        (n.x1, n.gain2, n.shift2),
        (n.x2, n.a3),
        *line_sends(n.a3),
    )
    s.a3_on, s.a3_on2, s.a3_in, s.middle = line_rows_steps(
        n.a3,
        lambda p, w, g: middle(p, w, g, inner),
        (n.full_mlp, n.whole_grad),
        (n.whole_mlp, n.active, n.hidden_low),
    )
    s.h3, s.h3_go, s.h3_on, s.h3_on2, s.h3_end = line_sums_steps(
        (n.hidden_low,),
        (n.full_mlp,),
        (0,),
        close_norm,
        (n.x2, n.gain2, n.c3),
        (n.e2, n.c2, n.norm2),
        *row_sends(n.c2),
    )
    s.g_mlp = (
        (n.whole_mlp, n.hidden_low, n.whole_grad, n.active),
        (n.g_both,),
        lambda a, u, b, v: (gradient_product([(a, u), (b, v)], 384),),
        (n.g_sum, n.g_both, to_sum),
    )

    def share(v):
        row = bit("row")
        first, second = halves(v)
        return jnp.where(row, second, first), jnp.where(row, first, second)

    def last_sum(a, b):
        total = a.astype(WIDE) + b.astype(WIDE)
        return total[:, :units], total[:, units:]

    s.g_mlp_row = ((n.g_sum,), (n.g_keep, n.g_give), share, (n.g_got, n.g_give, to_row))
    s.g_mlp_end = ((n.g_keep, n.g_got), (n.grad_up, n.grad_down), last_sum)
    s.act, s.act_go, s.act_on, s.act_on2, s.act_end = line_sums_steps(
        (n.active,),
        (n.full_mlp,),
        (1,),
        lambda a, b, c, x: ((x + plain_total(a, b, c)).astype(LOW),),
        (n.x2,),
        (n.act_local,),
    )
    s.c2_on, s.c2_in, s.d2 = rows_steps(
        n.c2, product_of(3, 1), (n.full_cross,), (n.whole_c2, n.d2)
    )
    s.mix2_back = (
        (n.query2, n.text_kv, n.d2),
        (n.dq2, n.dk2, n.dv2),
        lambda q, kv, d: attention_back((q, 0), (kv, 0), (kv, 1), d, places, False),
    )
    s.h2, s.h2_on, s.h2_end = sums_steps(
        (n.dq2,),
        (n.full_cross,),
        (0,),
        close_norm,
        (n.x1, n.gain1, n.e2),
        (n.e1, n.c1, n.norm1),
        *row_sends(n.c1),
    )
    s.g_cross, s.g_cross_far, s.g_cross_row, s.g_cross_end = gradients_steps(
        (n.whole_cross, n.dq2, n.whole_text, n.dk2, n.whole_text, n.dv2, n.whole_c2, n.mix2),
        [half] * 4,
        (n.grad_cq, n.grad_ck, n.grad_cv, n.grad_cout),
    )
    s.tg, s.tg_on, s.tg_end = sums_steps(
        (n.dk2, n.dv2),
        (n.full_cross, n.full_cross),
        (1, 2),
        lambda *v: (plain_total(*v),),
        (),
        (n.text_sum,),
    )
    s.c1_on, s.c1_in, s.d1 = rows_steps(
        n.c1, product_of(3, 1), (n.full_self,), (n.whole_c1, n.d1)
    )
    s.mix1_back = (
        (n.qkv, n.d1),
        (n.dq1, n.dk1, n.dv1),
        lambda q, d: attention_back((q, 0), (q, 1), (q, 2), d, places, True),
    )
    s.h1, s.h1_on, s.h1_end = sums_steps(
        (n.dq1, n.dk1, n.dv1),
        (n.full_self,) * 3,
        (0, 1, 2),
        close_norm,
        (n.x0, n.gain0, n.e1),
        (n.e0, n.c0, n.norm0),
    )
    s.g_self, s.g_self_far, s.g_self_row, s.g_self_end = gradients_steps(
        (n.whole_self, n.dq1, n.whole_self, n.dk1, n.whole_self, n.dv1, n.whole_c1, n.mix1),
        [half] * 4,
        (n.grad_q, n.grad_k, n.grad_v, n.grad_out),
    )

    def leave(*locals_):
        cut = [halves(regroup(v, 4)) for v in locals_]
        return *[v[0] for v in cut], jnp.concatenate([v[1].astype(LOW) for v in cut], axis=0)

    s.leave_act = ((n.act_local,), (n.keep_act, n.give_act), leave, (n.got_act, n.give_act, to_far))
    s.leave_text = ((n.text_sum,), (n.keep_text, n.give_text), leave, (n.got_text, n.give_text, to_far))
    s.sent = ((n.got_act, n.got_text), (n.got_act2, n.got_text2), keep)
    s.last = ((n.e0,), (n.keep_e, n.give_e), leave, (n.got_e, n.give_e, to_far))
    s.last_in = ((n.got_e,), (n.got_e2,), keep)

    def narrow(axis, outer, value):
        count, upper = value.shape[0], bit(axis)
        split = value.reshape(count, outer, 2, -1)
        low, high = [split[:, :, i].reshape(count, -1) for i in range(2)]
        return jnp.where(upper, high, low), jnp.where(upper, low, high)

    def sum_narrow(axis, outer):
        return lambda v, g: narrow(axis, outer, v + g)

    s.s0 = (
        (n.norm0, n.norm1, n.norm2),
        (n.k0, n.w0),
        lambda *v: narrow(axes[1], 8, regroup(jnp.concatenate(v, axis=0), 4)),
        (n.h0, n.w0, moves[1]),
    )
    s.s1 = ((n.k0, n.h0), (n.k1, n.w1), sum_narrow(axes[0], 8), (n.h1, n.w1, moves[0]))
    s.s2 = ((n.k1, n.h1), (n.k2, n.w2), sum_narrow(axes[2], 4), (n.h2, n.w2, moves[2]))
    s.s3 = ((n.k2, n.h2), (n.k3, n.w3), sum_narrow(axes[3], 2), (n.h3, n.w3, moves[3]))
    s.s4 = ((n.k3, n.h3), (n.k4, n.w4), sum_narrow(axes[4], 1), (n.h4, n.w4, moves[4]))
    s.s5 = ((n.k4, n.h4), (n.norm_sums,), lambda v, g: (v + g,))
    return (
        s.frames,
        s.w_self,
        s.n0,
        s.w_self_far,
        s.w_mlp,
        s.n1,
        s.frames_in,
        s.n2,
        s.n3,
        s.n4,
        s.w_mlp_all,
        s.norm0,
        s.w_self_all,
        s.trade,
        s.w_cross,
        s.a1_on,
        s.w_cross_far,
        s.a1_in,
        s.qkv,
        s.mix1,
        s.w_cross_all,
        s.w_mlp_go,
        s.x1,
        s.x1_on,
        s.both,
        s.text_go,
        s.x1_end,
        s.text_on,
        s.a2_on,
        s.text_in,
        s.text_all,
        s.c3_on,
        s.a2_in,
        s.text_kv,
        s.query2,
        s.mix2,
        s.x2,
        s.x2_on,
        s.c3_on2,
        s.x2_end,
        s.c3_in,
        s.c3_all,
        s.a3_on,
        s.a3_on2,
        s.a3_in,
        s.middle,
        s.h3,
        s.h3_go,
        s.g_mlp,
        s.h3_on,
        s.act,
        s.h3_on2,
        s.h3_end,
        s.c2_on,
        s.c2_in,
        s.act_go,
        s.d2,
        s.mix2_back,
        s.h2,
        s.g_cross,
        s.h2_on,
        s.h2_end,
        s.c1_on,
        s.g_mlp_row,
        s.act_on,
        s.c1_in,
        s.d1,
        s.mix1_back,
        s.g_self,
        s.g_cross_far,
        s.h1,
        s.act_on2,
        s.h1_on,
        s.g_mlp_end,
        s.act_end,
        s.g_cross_row,
        s.g_self_far,
        s.h1_end,
        s.leave_act,
        s.last,
        s.s0,
        s.tg,
        s.s1,
        s.tg_on,
        s.g_self_row,
        s.s2,
        s.tg_end,
        s.leave_text,
        s.s3,
        s.s4,
        s.g_cross_end,
        s.s5,
        s.last_in,
        s.sent,
        s.g_self_end,
    )


def on_device_pairs(
    frames,
    text_states,
    self_q,
    self_k,
    self_v,
    self_out,
    cross_q,
    cross_k,
    cross_v,
    cross_out,
    mlp_up,
    mlp_down,
    norm_gains,
    norm_shifts,
    cotangent,
):
    n = Name()
    values = {
        n.frames: frames,
        n.text_states: text_states,
        n.self_q: self_q,
        n.self_k: self_k,
        n.self_v: self_v,
        n.self_out: self_out.T,
        n.cross_q: cross_q,
        n.cross_k: cross_k,
        n.cross_v: cross_v,
        n.cross_out: cross_out.T,
        n.mlp_up: mlp_up,
        n.mlp_down: mlp_down.T,
        n.norm_gains: norm_gains,
        n.norm_shifts: norm_shifts,
        n.cotangent: cotangent,
    }
    order = plan_pairs(
        n, self_q.shape[1], mlp_up.shape[1], frames.shape[1], text_states.shape[1]
    )
    values = run_steps(values, order)
    far_bit = bit("far")

    def arrive(own, other):
        own, other = values[own], values[other].astype(values[own].dtype)
        return jnp.stack([jnp.where(far_bit, other, own), jnp.where(far_bit, own, other)])

    return (
        arrive(n.keep_act, n.got_act2),
        arrive(n.keep_e, n.got_e2),
        arrive(n.keep_text, n.got_text2),
        values[n.grad_q],
        values[n.grad_k],
        values[n.grad_v],
        values[n.grad_out].T,
        values[n.grad_cq],
        values[n.grad_ck],
        values[n.grad_cv],
        values[n.grad_cout].T,
        values[n.grad_up],
        values[n.grad_down].T,
        values[n.norm_sums][::2],
        values[n.norm_sums][1::2],
    )


def solution(mesh):
    paired = dict(mesh.shape) == {"dp": 8, "tensor": 4}
    names = ("row", "column", "core", "far", "near")
    dp, tensor = (names[:3], names[3:]) if paired else (("dp",), ("tensor",))
    rows = P(dp, tensor, None)
    into = P(dp, tensor)
    out_of = P(tensor, dp)
    norms = P(None, dp + tensor)
    weights = (into, into, into, out_of, into, into, into, out_of, into, out_of)
    return jax.shard_map(
        on_device_pairs if paired else on_device,
        mesh=Mesh(mesh.devices.reshape((2,) * 5), names) if paired else mesh,
        in_specs=(rows, rows, *weights, norms, norms, rows),
        out_specs=(rows, rows, rows, *weights, norms, norms),
        check_vma=False,
    )
```
